32 devices in a mesh: pipe: 8 (over z, y), dp: 4 (over x, core).
Axes of the slice: x: 2, y: 2, z: 4, core: 2. Of those that a mesh axis runs over, the one named last changes fastest.
Arguments:
- grad_output: bfloat16 [512, 8192], P('dp'), may hold values from -6 to 6
- hidden: bfloat16 [512, 14336], P('dp', 'pipe'), may hold values from -6 to 6
- next_hidden: bfloat16 [512, 14336], P('dp', 'pipe'), may hold values from -6 to 6
- master: float32 [14336, 8192], P('pipe', 'dp'), may hold values from -0.046875 to 0.046875
- moment: float32 [14336, 8192], P('pipe', 'dp'), may hold values from -24 to 24
- second_moment: float32 [14336, 8192], P('pipe', 'dp'), may hold values from 5 to 100
Outputs:
- update: float32 [14336, 8192], P('pipe', 'dp')
- upstream_grad: bfloat16 [512, 14336], P('dp', 'pipe')
- next_output: bfloat16 [512, 8192], P('pipe', 'dp')
The draws below stay inside these ranges and needn't reach their ends.
All inputs are finite; a program needn't handle non-finite values.
Results may differ from the reference program's by a relative error of at most 0.005.
Values may be sent and summed in bfloat16 or wider, within the bound.
A program may use at most 256 MiB of HBM per device.

```python
import math
import jax
import jax.numpy as jnp
from jax import lax

D = 8192
FF = 14336
TOKENS = 512


def levels(key, dims, cuts, low, high):
    level = 1.0
    for dim, shards_of in cuts:
        steps = jax.random.uniform(jax.random.fold_in(jax.random.fold_in(key, 6), dim), (shards_of,), jnp.float32, low / len(cuts), high / len(cuts))
        level = level * jnp.repeat(jnp.exp(steps), dims[dim] // shards_of).reshape((-1,) + (1,) * (len(dims) - 1 - dim))
    return level


def bell_draw(key, shape, width, limit, split=(), dtype=jnp.bfloat16):
    level = levels(key, shape, split, -0.22, 0.18) if split else 1.0
    result = jax.random.normal(key, shape, jnp.float32) * width * level
    return jnp.minimum(jnp.maximum(result, -limit), limit).astype(dtype)


def setup_inputs(seed: int = 0) -> dict:
    key_list = jax.random.split(jax.random.key(seed), 7)
    grad_output = bell_draw(key_list[0], (TOKENS, D), 1.0, 6.0, ((0, 4),))
    hidden = bell_draw(key_list[1], (TOKENS, FF), 1.0, 6.0, ((0, 4), (1, 8)))
    next_hidden = bell_draw(key_list[2], (TOKENS, FF), 1.0, 6.0, ((0, 4), (1, 8)))
    master = bell_draw(key_list[3], (FF, D), FF ** -0.5, 0.046875, ((0, 8), (1, 4)), jnp.float32)
    moment = bell_draw(key_list[4], (FF, D), 4.0, 24.0, ((0, 8), (1, 4)), jnp.float32)
    second_moment = jnp.clip(jnp.exp(math.log(100.0) - 2.9957323 * jax.random.uniform(key_list[5], (FF, D), jnp.float32) ** levels(key_list[5], (FF, D), ((0, 8), (1, 4)), -0.2, 0.2)), 5.0, 100.0)
    return {"grad_output": grad_output, "hidden": hidden, "next_hidden": next_hidden, "master": master, "moment": moment, "second_moment": second_moment}


beta_one = 0.9
beta_two = 0.95
corr_one = 1.0 - 0.9 ** 10
corr_two = 1.0 - 0.95 ** 10
learn_rate = 0.005
decay_rate = 0.1
epsilon = 1e-08

def reference(grad_output, hidden, next_hidden, master, moment, second_moment):
    weights_low = master.astype(jnp.bfloat16)
    upstream_grad = lax.dot_general(grad_output, weights_low, (((1,), (1,)), ((), ())), preferred_element_type=jnp.float32).astype(jnp.bfloat16)
    gradient = lax.dot_general(hidden, grad_output, (((0,), (0,)), ((), ())), preferred_element_type=jnp.float32)
    moment_new = beta_one * moment + (1.0 - beta_one) * gradient
    second_new = beta_two * second_moment + (1.0 - beta_two) * gradient * gradient
    update = -(moment_new / corr_one / (jnp.sqrt(second_new / corr_two) + epsilon) + decay_rate * master)
    fresh_low = (master + learn_rate * update).astype(jnp.bfloat16)
    next_output = jnp.dot(next_hidden, fresh_low, preferred_element_type=jnp.float32).astype(jnp.bfloat16)
    return (update, upstream_grad, next_output)
```

```python
import functools
import math

import jax
import jax.numpy as jnp
from jax import lax
from jax.experimental import pallas as pl
from jax.experimental.pallas import tpu as pltpu
from jax.sharding import PartitionSpec as P

beta_one = 0.9
beta_two = 0.95
corr_one = 1.0 - 0.9**10
corr_two = 1.0 - 0.95**10
learn_rate = 0.005
decay_rate = 0.1
epsilon = 1e-08

f32 = jnp.float32
bf16 = jnp.bfloat16
MESH = pl.DeviceIdType.MESH
ALL = slice(None)


def remote(src, dst, send, recv, pipe, dp):
    return pltpu.make_async_remote_copy(
        src_ref=src, dst_ref=dst, send_sem=send, recv_sem=recv,
        device_id=(pipe, dp), device_id_type=MESH,
    )


def greet(partners):
    barrier = pltpu.get_barrier_semaphore()
    for partner in partners:
        pl.semaphore_signal(barrier, inc=1, device_id=partner, device_id_type=MESH)
    pl.semaphore_wait(barrier, len(partners))


def adam(w, m, s, grad):
    top = (-beta_one / corr_one) * m + (-(1.0 - beta_one) / corr_one) * grad
    var = (beta_two / corr_two) * s + ((1.0 - beta_two) / corr_two) * (grad * grad)
    root = lax.rsqrt(var)
    below = var * root + epsilon
    inverse = root * (2.0 - below * root)
    return top * inverse - decay_rate * w


class Plan:
    def __init__(self, n_pipe, n_dp, rows, ff, width):
        self.n_pipe, self.n_dp, self.rows, self.ff, self.width = n_pipe, n_dp, rows, ff, width
        self.chips = n_dp // 2
        self.tokens = n_dp * rows
        self.few = self.tokens // n_pipe
        self.share = 4 if n_pipe % 4 == 0 else 1
        self.low = int(math.log2(n_pipe // self.chips))
        self.high = int(math.log2(self.chips))
        self.chunk = 256 if ff % 256 == 0 else 128
        self.chunks = ff // self.chunk
        self.slots = min(3, self.chunks)
        self.tile = 512 if width % 512 == 0 else width
        self.pieces = 8 if width % 2048 == 0 else 4 if width % 512 == 0 else 1
        self.cw = width // self.pieces


def scratch_of(p):
    dma = pltpu.SemaphoreType.DMA
    v = pltpu.VMEM
    mates = max(p.share - 1, 1)
    out = dict(
        w=v((p.ff, p.width), f32),
        s=v((p.slots, p.chunk, p.width), f32),
        fresh=v((p.ff, p.width), bf16),
        cols=v((p.n_dp, p.rows, p.width), bf16),
        h=v((p.n_dp, p.rows, p.ff), bf16),
        nh=v((p.n_dp, p.rows, p.ff), bf16),
        turned=v((p.chunk, p.tokens), bf16),
        up=v((p.chips, 2, p.rows, p.ff), bf16),
        up_in=v((p.chips, p.rows, p.ff), bf16),
        up_mid=v((p.chips, p.rows, p.ff), bf16),
        up_far=v((p.chips, p.rows, p.ff), bf16),
        nxt=v((p.chips,) + (2,) * p.low + (p.few, p.width), bf16),
        acc=v((p.chips, p.few, p.width), f32),
        loc=dma((3,)), m_l=dma((p.chunks,)), w_l=dma((p.chunks,)), s_l=dma((p.slots,)),
        sib_s=dma((3,)), sib_r=dma((3,)),
        g_s=dma((p.chips, 2)), g_r=dma((p.chips, 2)),
        gf_s=dma((p.chips, 2, mates)), gf_r=dma((p.chips, 2, mates)),
        h_s=dma((p.chips, p.chunks)), h_r=dma((p.chips, p.chunks)),
        hf_s=dma((p.chips, p.chunks)), hf_r=dma((p.chips, p.chunks)),
        n_s=dma((p.chips, 2)), n_r=dma((p.chips, 2)),
        nf_s=dma((p.chips, 2)), nf_r=dma((p.chips, 2)),
        us_s=dma((p.chips, p.chunks)), us_r=dma((p.chips, p.chunks)),
        uf_s=dma((p.chips, p.chunks)), uf_r=dma((p.chips, p.chunks)),
        r_s=dma((p.chips, p.low, p.pieces)), r_r=dma((p.chips, p.low, p.pieces)),
        t_s=dma((p.high, p.pieces)), t_r=dma((p.high, p.pieces)),
    )
    for j in range(p.low):
        shape = (p.chips,) + (2,) * (p.low - 1 - j) + (p.few, p.width)
        out[f"recv{j}"] = v(shape, bf16)
        if j:
            out[f"send{j}"] = v(shape, bf16)
            out[f"keep{j}"] = v(shape, f32)
    for j in range(p.high):
        shape = (p.chips >> (j + 1), p.few, p.width)
        out[f"top_send{j}"] = v(shape, bf16)
        out[f"top_recv{j}"] = v(shape, bf16)
    return out


def whole_kernel(p, names, g, hid, nhid, master, moment, second, upd, up_out, next_out, *refs):
    b = dict(zip(names, refs))
    cols, h, nh, w_v, s_v, fresh, up = (b[n] for n in ("cols", "h", "nh", "w", "s", "fresh", "up"))
    pipe, dp = lax.axis_index("pipe"), lax.axis_index("dp")
    chips, rows, width, ch = p.chips, p.rows, p.width, p.chunk
    chip, core = dp // 2, dp % 2
    sib = chip * 2 + 1 - core
    ahead = [(chip + o) % chips for o in range(chips)]
    behind = [(chip + chips - o) % chips for o in range(chips)]
    bits = p.low + p.high
    bit = [(pipe // 2**i) % 2 for i in range(bits)]

    def flip(f):
        at = pipe
        for i in range(bits):
            if (f >> i) & 1:
                at = at + (1 - 2 * bit[i]) * 2**i
        return at

    def columns(d):
        return pl.ds(pl.multiple_of(d * width, width), width)

    def part_of(c):
        return pl.ds(pl.multiple_of(c * ch, ch), ch)

    own_g = pltpu.make_async_copy(g.at[:, columns(dp)], cols.at[dp], b["loc"].at[0])
    own_h = pltpu.make_async_copy(hid, h.at[dp], b["loc"].at[1])
    own_n = pltpu.make_async_copy(nhid, nh.at[dp], b["loc"].at[2])

    def load_m(c):
        return pltpu.make_async_copy(moment.at[part_of(c)], upd.at[part_of(c)], b["m_l"].at[c])

    def load_w(c):
        return pltpu.make_async_copy(master.at[part_of(c)], w_v.at[part_of(c)], b["w_l"].at[c])

    def load_s(c, slot):
        return pltpu.make_async_copy(second.at[part_of(c)], s_v.at[slot], b["s_l"].at[slot])

    for c in (own_g, own_h):
        c.start()
    for c in range(p.chunks):
        load_m(c).start()
        load_w(c).start()
        if c < p.slots:
            load_s(c, c).start()
    own_n.start()

    partners = [(pipe, sib)]
    partners += [(pipe, ahead[o] * 2 + (core + e) % 2) for o in range(1, chips) for e in range(2)]
    flips = sorted(set(range(1, p.share)) | {2**i for i in range(bits)})
    partners += [(flip(f), dp) for f in flips]
    greet(partners)

    part = rows // p.share
    mine = pl.ds(pl.multiple_of(pipe % p.share * part, part), part)
    cross = {}
    for o in range(1, chips):
        for e in range(2):
            d = ahead[o] * 2 + (core + e) % 2
            cross[o, e] = remote(g.at[mine, columns(d)], cols.at[dp, mine],
                                 b["g_s"].at[o, e], b["g_r"].at[o, e], pipe, d)
            cross[o, e].start()

    def hop(o, c):
        return remote(hid.at[:, part_of(c)], h.at[dp, :, part_of(c)],
                      b["h_s"].at[o, c], b["h_r"].at[o, c], pipe, ahead[o] * 2 + core)

    def pass_on(o, c):
        block = h.at[behind[o] * 2 + core, :, part_of(c)]
        return remote(block, block, b["hf_s"].at[o, c], b["hf_r"].at[o, c], pipe, sib)

    half = rows // 2

    def later(o, i):
        some = pl.ds(i * half, half)
        return remote(nhid.at[some], nh.at[dp, some], b["n_s"].at[o, i], b["n_r"].at[o, i],
                      pipe, ahead[o] * 2 + core)

    def pass_later(o, i):
        block = nh.at[behind[o] * 2 + core, pl.ds(i * half, half)]
        return remote(block, block, b["nf_s"].at[o, i], b["nf_r"].at[o, i], pipe, sib)

    side = [
        remote(g.at[:, columns(sib)], cols.at[dp], b["sib_s"].at[0], b["sib_r"].at[0], pipe, sib),
        remote(hid, h.at[dp], b["sib_s"].at[1], b["sib_r"].at[1], pipe, sib),
        remote(nhid, nh.at[dp], b["sib_s"].at[2], b["sib_r"].at[2], pipe, sib),
    ]
    for c in range(p.chunks):
        for o in range(1, chips):
            hop(o, c).start()
    for c in side:
        c.start()
    for o in range(1, chips):
        for i in range(2):
            later(o, i).start()

    passed = []
    for o in range(1, chips):
        for e in range(2):
            cross[o, e].wait_recv()
            block = cols.at[behind[o] * 2 + (core + e) % 2, mine]
            for f in range(1, p.share):
                c = remote(block, block, b["gf_s"].at[o, e, f - 1], b["gf_r"].at[o, e, f - 1], flip(f), dp)
                c.start()
                passed.append(c)
    for o in range(1, chips):
        hop(o, 0).wait_recv()
        pass_on(o, 0).start()
    own_g.wait()
    own_h.wait()
    side[0].wait_recv()
    side[1].wait_recv()
    for c in passed:
        c.wait_recv()

    @pl.loop(0, p.chunks)
    def _(c):
        r = part_of(c)
        slot = lax.rem(c, p.slots)

        @pl.when(c + 1 < p.chunks)
        def _():
            for o in range(1, chips):
                hop(o, c + 1).wait_recv()
                pass_on(o, c + 1).start()

        load_m(c).wait()
        load_w(c).wait()
        load_s(c, slot).wait()
        for o in range(1, chips):
            pass_on(o, c).wait_recv()
        b["turned"][...] = h[:, :, r].reshape(p.tokens, ch).T
        for n in range(0, width, p.tile):
            k = pl.ds(n, p.tile)
            grad = jnp.dot(b["turned"][...], cols[:, :, k].reshape(p.tokens, p.tile),
                           preferred_element_type=f32)
            w = w_v[r, k]
            update = adam(w, upd[r, k], s_v[slot, :, k], grad)
            upd[r, k] = update
            fresh[r, k] = (w + learn_rate * update).astype(bf16)

        @pl.when(c + p.slots < p.chunks)
        def _():
            load_s(c + p.slots, slot).start()

    low, cw = p.low, p.cw
    recv = [b[f"recv{j}"] for j in range(low)]
    send = [b.get(f"send{j}") for j in range(low)]
    keep = [b.get(f"keep{j}") for j in range(low)]
    nxt, acc = b["nxt"], b["acc"]

    def order_of(o, k):
        order = list(range(low))
        if o == 0 and k % 2 and low > 1:
            order[0], order[1] = order[1], order[0]
        return order

    def pick(o, k, j, value):
        left = sorted(order_of(o, k)[j:], reverse=True)
        at = left.index(order_of(o, k)[j])
        return (ALL,) * at + (value,) + (ALL,) * (len(left) - 1 - at)

    def tail(k):
        return (ALL, pl.ds(k * cw, cw))

    def spot(o, j, k):
        return (o,) + (ALL,) * (low - 1 - j) + tail(k)

    flights = {}

    def launch(o, j, k, src):
        turn = order_of(o, k)[j]
        flights[o, j, k] = remote(src, recv[j].at[spot(o, j, k)], b["r_s"].at[o, j, k],
                                  b["r_r"].at[o, j, k], flip(2**turn), dp)
        flights[o, j, k].start()

    def multiply(o, k):
        t = behind[o]
        left = nh[pl.ds(t * 2, 2)].reshape(2 * rows, p.ff)
        product = jnp.dot(left, fresh[:, pl.ds(k * cw, cw)], preferred_element_type=f32).astype(bf16)
        nxt[(t,) + (ALL,) * low + tail(k)] = product.reshape((2,) * low + (p.few, cw))
        launch(o, 0, k, nxt.at[(t,) + pick(o, k, 0, 1 - bit[order_of(o, k)[0]]) + tail(k)])

    def combine(o, j, k):
        flights[o, j, k].wait_recv()

        def summed(index):
            if j == 0:
                mine = pick(o, k, 0, bit[order_of(o, k)[0]])
                full, i = [], iter(index)
                for m in mine:
                    full.append(next(i) if isinstance(m, slice) else m)
                kept = nxt[(behind[o],) + tuple(full) + tail(k)]
            else:
                kept = keep[j][(o,) + index + tail(k)]
            return kept.astype(f32) + recv[j][(o,) + index + tail(k)].astype(f32)

        if j < low - 1:
            turn = bit[order_of(o, k)[j + 1]]
            send[j + 1][spot(o, j + 1, k)] = summed(pick(o, k, j + 1, 1 - turn)).astype(bf16)
            launch(o, j + 1, k, send[j + 1].at[spot(o, j + 1, k)])
            keep[j + 1][spot(o, j + 1, k)] = summed(pick(o, k, j + 1, turn))
        else:
            acc[(behind[o],) + tail(k)] = summed(())

    tops = {}
    starts = [0]
    for j in range(p.high):
        starts.append(starts[j] + bit[low + p.high - 1 - j] * (chips >> (j + 1)))

    def top_launch(j, k):
        count = chips >> (j + 1)
        turn = low + p.high - 1 - j
        away = starts[j] + (1 - bit[turn]) * count
        b[f"top_send{j}"][(ALL,) + tail(k)] = acc[(pl.ds(away, count),) + tail(k)].astype(bf16)
        tops[j, k] = remote(b[f"top_send{j}"].at[(ALL,) + tail(k)], b[f"top_recv{j}"].at[(ALL,) + tail(k)],
                            b["t_s"].at[j, k], b["t_r"].at[j, k], flip(2**turn), dp)
        tops[j, k].start()

    def top_combine(j, k):
        count = chips >> (j + 1)
        tops[j, k].wait_recv()
        kept = acc[(pl.ds(starts[j + 1], count),) + tail(k)]
        total = kept + b[f"top_recv{j}"][(ALL,) + tail(k)].astype(f32)
        if j < p.high - 1:
            acc[(pl.ds(starts[j + 1], count),) + tail(k)] = total
            top_launch(j + 1, k)
        else:
            next_out[tail(k)] = total.reshape(p.few, cw).astype(bf16)

    def near(o, c):
        return remote(up.at[ahead[o], 1 - core, :, part_of(c)], b["up_in"].at[o, :, part_of(c)],
                      b["us_s"].at[o, c], b["us_r"].at[o, c], pipe, sib)

    def far(o, c):
        return remote(b["up_mid"].at[o, :, part_of(c)], b["up_far"].at[o, :, part_of(c)],
                      b["uf_s"].at[o, c], b["uf_r"].at[o, c], pipe, ahead[o] * 2 + core)

    own_n.wait()
    side[2].wait_recv()
    for k in range(p.pieces):
        multiply(0, k)

    @pl.loop(0, p.chunks)
    def _(c):
        r = part_of(c)
        product = lax.dot_general(
            cols[...].reshape(p.tokens, width), w_v[r, :].astype(bf16),
            (((1,), (1,)), ((), ())), preferred_element_type=f32,
        ).astype(bf16)
        up[:, :, :, r] = product.reshape(chips, 2, rows, ch)
        for o in range(chips):
            near(o, c).start()

    for k in range(p.pieces):
        combine(0, 0, k)

    @pl.loop(0, p.chunks)
    def _(c):
        r = part_of(c)
        for o in range(1, chips):
            near(o, c).wait_recv()
            b["up_mid"][o, :, r] = (up[ahead[o], core, :, r].astype(f32)
                                    + b["up_in"][o, :, r].astype(f32)).astype(bf16)
            far(o, c).start()

    for o in range(1, chips):
        for i in range(2):
            later(o, i).wait_recv()
            pass_later(o, i).start()
        for i in range(2):
            pass_later(o, i).wait_recv()
        for k in range(p.pieces):
            multiply(o, k)
        for j in range(1, low):
            for k in range(p.pieces):
                combine(o - 1, j, k)
        for k in range(p.pieces):
            combine(o, 0, k)
    last = chips - 1
    for k in range(p.pieces):
        for j in range(1, low):
            combine(last, j, k)
        if p.high:
            top_launch(0, k)

    @pl.loop(0, p.chunks)
    def _(c):
        r = part_of(c)
        near(0, c).wait_recv()
        total = up[chip, core, :, r].astype(f32) + b["up_in"][0, :, r].astype(f32)
        for o in range(1, chips):
            far(o, c).wait_recv()
            total = total + b["up_far"][o, :, r].astype(f32)
        up_out[:, r] = total.astype(bf16)

    for j in range(p.high):
        for k in range(p.pieces):
            top_combine(j, k)

    for c in list(cross.values()) + side + passed + list(flights.values()) + list(tops.values()):
        c.wait_send()
    for o in range(1, chips):
        for i in range(2):
            later(o, i).wait_send()
            pass_later(o, i).wait_send()

    @pl.loop(0, p.chunks)
    def _(c):
        near(0, c).wait_send()
        for o in range(1, chips):
            hop(o, c).wait_send()
            pass_on(o, c).wait_send()
            near(o, c).wait_send()
            far(o, c).wait_send()


def place_kernel(a, b, c, x, y, z, sems):
    copies = [pltpu.make_async_copy(s, d, sems.at[i]) for i, (s, d) in enumerate(((a, x), (b, y), (c, z)))]
    for copy in copies:
        copy.start()
    for copy in copies:
        copy.wait()


def on_device(n_pipe, n_dp, grad_output, hidden, next_hidden, master, moment, second_moment):
    rows, ff = hidden.shape
    width = master.shape[1]
    p = Plan(n_pipe, n_dp, rows, ff, width)
    hbm = pl.BlockSpec(memory_space=pltpu.HBM)
    vmem = pl.BlockSpec(memory_space=pltpu.VMEM)
    shapes = [((ff, width), f32), ((rows, ff), bf16), ((p.few, width), bf16)]
    scratch = scratch_of(p)
    held = pl.pallas_call(
        functools.partial(whole_kernel, p, list(scratch)),
        out_shape=[pltpu.VMEM(s, t) for s, t in shapes],
        in_specs=[hbm] * 6,
        out_specs=[vmem] * 3,
        scratch_shapes=list(scratch.values()),
        compiler_params=pltpu.CompilerParams(
            collective_id=1, has_side_effects=True, vmem_limit_bytes=48 << 20
        ),
        cost_estimate=pl.CostEstimate(
            flops=6 * p.tokens * ff * width, bytes_accessed=16 * ff * width, transcendentals=ff * width
        ),
        name="whole_step",
    )(grad_output, hidden, next_hidden, master, moment, second_moment)
    held = [pltpu.with_memory_space_constraint(a, pltpu.VMEM) for a in held]
    return tuple(pl.pallas_call(
        place_kernel,
        out_shape=[jax.ShapeDtypeStruct(s, t) for s, t in shapes],
        in_specs=[vmem] * 3,
        out_specs=[hbm] * 3,
        scratch_shapes=[pltpu.SemaphoreType.DMA((3,))],
        compiler_params=pltpu.CompilerParams(has_side_effects=True, vmem_limit_bytes=1 << 20),
        name="place_outputs",
    )(*held))


def solution(mesh):
    in_specs = (
        P("dp", None),
        P("dp", "pipe"),
        P("dp", "pipe"),
        P("pipe", "dp"),
        P("pipe", "dp"),
        P("pipe", "dp"),
    )
    out_specs = (P("pipe", "dp"), P("dp", "pipe"), P("pipe", "dp"))

    def run(grad_output, hidden, next_hidden, master, moment, second_moment):
        f = functools.partial(on_device, mesh.shape["pipe"], mesh.shape["dp"])
        update, upstream, next_out = jax.shard_map(
            f, mesh=mesh, in_specs=in_specs, out_specs=out_specs, check_vma=False,
        )(grad_output, hidden, next_hidden, master, moment, second_moment)
        return update, upstream, next_out

    return run
```

```python
import functools
import math

import jax
import jax.numpy as jnp
from jax import lax
from jax.experimental import pallas as pl
from jax.experimental.pallas import tpu as pltpu
from jax.sharding import PartitionSpec as P

beta_one = 0.9
beta_two = 0.95
corr_one = 1.0 - 0.9**10
corr_two = 1.0 - 0.95**10
learn_rate = 0.005
decay_rate = 0.1
epsilon = 1e-08

f32 = jnp.float32
bf16 = jnp.bfloat16
MESH = pl.DeviceIdType.MESH
ALL = slice(None)


def remote(src, dst, send, recv, pipe, dp):
    return pltpu.make_async_remote_copy(
        src_ref=src, dst_ref=dst, send_sem=send, recv_sem=recv,
        device_id=(pipe, dp), device_id_type=MESH,
    )


def greet(partners):
    barrier = pltpu.get_barrier_semaphore()
    for partner in partners:
        pl.semaphore_signal(barrier, inc=1, device_id=partner, device_id_type=MESH)
    pl.semaphore_wait(barrier, len(partners))


def adam(w, m, s, grad):
    top = (-beta_one / corr_one) * m + (-(1.0 - beta_one) / corr_one) * grad
    var = (beta_two / corr_two) * s + ((1.0 - beta_two) / corr_two) * (grad * grad)
    root = lax.rsqrt(var)
    below = var * root + epsilon
    inverse = root * (2.0 - below * root)
    return top * inverse - decay_rate * w


class Plan:
    def __init__(self, n_pipe, n_dp, rows, ff, width):
        self.n_pipe, self.n_dp, self.rows, self.ff, self.width = n_pipe, n_dp, rows, ff, width
        self.chips = n_dp // 2
        self.tokens = n_dp * rows
        self.few = self.tokens // n_pipe
        self.share = 4 if n_pipe % 4 == 0 else 1
        self.low = int(math.log2(n_pipe // self.chips))
        self.high = int(math.log2(self.chips))
        self.chunk = 256 if ff % 256 == 0 else 128
        self.chunks = ff // self.chunk
        self.halves = 2 if width % 256 == 0 else 1
        self.hw = width // self.halves
        self.slots = min(4, self.chunks)
        self.early = min(3, self.chunks // 2)
        self.tile = 512 if self.hw % 512 == 0 else self.hw
        self.pieces = 8 if width % 2048 == 0 else 4 if width % 512 == 0 else 1
        self.cw = width // self.pieces


def scratch_of(p):
    dma = pltpu.SemaphoreType.DMA
    v = pltpu.VMEM
    out = dict(
        w=v((p.ff, p.width), f32),
        m=v((p.slots, p.chunk, p.hw), f32),
        s=v((p.slots, p.chunk, p.hw), f32),
        fresh=v((p.ff, p.width), bf16),
        cols=v((p.n_dp, p.rows, p.width), bf16),
        h=v((p.n_dp, p.rows, p.ff), bf16),
        nh=v((p.n_dp, p.rows, p.ff), bf16),
        turned=v((p.chunk, p.tokens), bf16),
        up=v((p.chips, 2, p.rows, p.ff), bf16),
        up_in=v((p.chips, p.rows, p.ff), bf16),
        up_mid=v((p.chips, p.rows, p.ff), bf16),
        up_far=v((p.chips, p.rows, p.ff), bf16),
        nxt=v((p.chips,) + (2,) * p.low + (p.few, p.width), bf16),
        acc=v((p.chips, p.few, p.width), f32),
        loc=dma((3,)), m_l=dma((p.slots,)), w_l=dma((p.halves, p.chunks)), s_l=dma((p.slots,)),
        sib_s=dma((3,)), sib_r=dma((3,)),
        g_s=dma((p.chips, 2, p.halves)), g_r=dma((p.chips, 2, p.halves)),
        gf_s=dma((p.chips, 2, p.halves, 4)), gf_r=dma((p.chips, 2, p.halves, 4)),
        h_s=dma((p.chips, p.chunks)), h_r=dma((p.chips, p.chunks)),
        hf_s=dma((p.chips, p.chunks)), hf_r=dma((p.chips, p.chunks)),
        n_s=dma((p.chips, 2)), n_r=dma((p.chips, 2)),
        nf_s=dma((p.chips, 2)), nf_r=dma((p.chips, 2)),
        us_s=dma((p.chips, p.chunks)), us_r=dma((p.chips, p.chunks)),
        uf_s=dma((p.chips, p.chunks)), uf_r=dma((p.chips, p.chunks)),
        r_s=dma((p.chips, p.low, p.pieces)), r_r=dma((p.chips, p.low, p.pieces)),
        t_s=dma((p.high, p.pieces)), t_r=dma((p.high, p.pieces)),
    )
    for j in range(p.low):
        shape = (p.chips,) + (2,) * (p.low - 1 - j) + (p.few, p.width)
        out[f"recv{j}"] = v(shape, bf16)
        if j:
            out[f"send{j}"] = v(shape, bf16)
            out[f"keep{j}"] = v(shape, f32)
    for j in range(p.high):
        shape = (p.chips >> (j + 1), p.few, p.width)
        out[f"top_send{j}"] = v(shape, bf16)
        out[f"top_recv{j}"] = v(shape, bf16)
    return out


def whole_kernel(p, names, g, hid, nhid, master, moment, second, upd, up_out, next_out, *refs):
    b = dict(zip(names, refs))
    cols, h, nh, fresh, up = (b[n] for n in ("cols", "h", "nh", "fresh", "up"))
    w_v, m_v, s_v = b["w"], b["m"], b["s"]
    pipe, dp = lax.axis_index("pipe"), lax.axis_index("dp")
    chips, rows, width, ch = p.chips, p.rows, p.width, p.chunk
    chip, core = dp // 2, dp % 2
    sib = chip * 2 + 1 - core
    ahead = [(chip + o) % chips for o in range(chips)]
    behind = [(chip + chips - o) % chips for o in range(chips)]
    bits = p.low + p.high
    bit = [(pipe // 2**i) % 2 for i in range(bits)]

    def flip(f):
        at = pipe
        for i in range(bits):
            if (f >> i) & 1:
                at = at + (1 - 2 * bit[i]) * 2**i
        return at

    def columns(d):
        return pl.ds(pl.multiple_of(d * width, width), width)

    def part_of(c):
        return pl.ds(pl.multiple_of(c * ch, ch), ch)

    own_g = pltpu.make_async_copy(g.at[:, columns(dp)], cols.at[dp], b["loc"].at[0])
    own_h = pltpu.make_async_copy(hid, h.at[dp], b["loc"].at[1])
    own_n = pltpu.make_async_copy(nhid, nh.at[dp], b["loc"].at[2])

    def side_of(q):
        return pl.ds(q * p.hw, p.hw)

    def load_w(q, c):
        at = (part_of(c), side_of(q))
        return pltpu.make_async_copy(master.at[at], w_v.at[at], b["w_l"].at[q, c])

    turns = p.halves * p.chunks

    def load_states(i):
        slot = i % p.slots
        at = (part_of(i % p.chunks), pl.ds(pl.multiple_of(i // p.chunks * p.hw, p.hw), p.hw))
        return [
            pltpu.make_async_copy(moment.at[at], m_v.at[slot], b["m_l"].at[slot]),
            pltpu.make_async_copy(second.at[at], s_v.at[slot], b["s_l"].at[slot]),
        ]

    for c in (own_g, own_h):
        c.start()
    for i in range(turns):
        load_w(i // p.chunks, i % p.chunks).start()
        if i < p.slots:
            for c in load_states(i):
                c.start()
        if i == p.chunks:
            own_n.start()

    partners = [(pipe, sib)]
    partners += [(pipe, ahead[o] * 2 + (core + e) % 2) for o in range(1, chips) for e in range(2)]
    flips = sorted(set(range(1, p.share)) | {2**i for i in range(bits)})
    partners += [(flip(f), dp) for f in flips]
    greet(partners)

    part = rows // p.share
    place = pipe % p.share

    def rows_of(at):
        return pl.ds(pl.multiple_of(at * part, part), part)

    def piece(d, q):
        return pl.ds(pl.multiple_of(d * width + q * p.hw, p.hw), p.hw)

    cross = {}
    for q in range(p.halves):
        for o in range(1, chips):
            for e in range(2):
                d = ahead[o] * 2 + (core + e) % 2
                cross[q, o, e] = remote(g.at[rows_of(place), piece(d, q)],
                                        cols.at[dp, rows_of(place), side_of(q)],
                                        b["g_s"].at[o, e, q], b["g_r"].at[o, e, q], pipe, d)
                cross[q, o, e].start()

    def shared(q, o, e, f):
        block = cols.at[behind[o] * 2 + (core + e) % 2, rows_of(place), side_of(q)]
        return remote(block, block, b["gf_s"].at[o, e, q, f], b["gf_r"].at[o, e, q, f], flip(f), dp)

    def hop(o, c):
        return remote(hid.at[:, part_of(c)], h.at[dp, :, part_of(c)],
                      b["h_s"].at[o, c], b["h_r"].at[o, c], pipe, ahead[o] * 2 + core)

    def pass_on(o, c):
        block = h.at[behind[o] * 2 + core, :, part_of(c)]
        return remote(block, block, b["hf_s"].at[o, c], b["hf_r"].at[o, c], pipe, sib)

    half = rows // 2

    def later(o, i):
        some = pl.ds(i * half, half)
        return remote(nhid.at[some], nh.at[dp, some], b["n_s"].at[o, i], b["n_r"].at[o, i],
                      pipe, ahead[o] * 2 + core)

    def pass_later(o, i):
        block = nh.at[behind[o] * 2 + core, pl.ds(i * half, half)]
        return remote(block, block, b["nf_s"].at[o, i], b["nf_r"].at[o, i], pipe, sib)

    side = [
        remote(g.at[:, columns(sib)], cols.at[dp], b["sib_s"].at[0], b["sib_r"].at[0], pipe, sib),
        remote(hid, h.at[dp], b["sib_s"].at[1], b["sib_r"].at[1], pipe, sib),
        remote(nhid, nh.at[dp], b["sib_s"].at[2], b["sib_r"].at[2], pipe, sib),
    ]
    for c in range(p.chunks):
        for o in range(1, chips):
            hop(o, c).start()
    for c in side:
        c.start()
    for o in range(1, chips):
        for i in range(2):
            later(o, i).start()

    passed = {q: [] for q in range(p.halves)}
    for key in cross:
        q, o, e = key
        cross[key].wait_recv()
        for f in range(1, p.share):
            c = shared(q, o, e, f)
            c.start()
            passed[q].append(c)

    def up_chunk(c):
        r = part_of(c)
        product = lax.dot_general(
            cols[...].reshape(p.tokens, width), w_v[r, :].astype(bf16),
            (((1,), (1,)), ((), ())), preferred_element_type=f32,
        ).astype(bf16)
        up[:, :, :, r] = product.reshape(chips, 2, rows, ch)
        for o in range(chips):
            near(o, c).start()

    def step(q, c):
        r = part_of(c)
        i = q * p.chunks + c
        slot = lax.rem(i, p.slots)
        if q == 0:
            load_w(q, c).wait()
        else:
            @pl.when(c >= p.early)
            def _():
                load_w(q, c).wait()

        for copy in load_states(i):
            copy.wait()
        b["turned"][...] = h[:, :, r].reshape(p.tokens, ch).T
        for n in range(0, p.hw, p.tile):
            k = pl.ds(q * p.hw + n, p.tile)
            grad = jnp.dot(b["turned"][...], cols[:, :, k].reshape(p.tokens, p.tile),
                           preferred_element_type=f32)
            w = w_v[r, k]
            update = adam(w, m_v[slot, :, pl.ds(n, p.tile)], s_v[slot, :, pl.ds(n, p.tile)], grad)
            upd[r, k] = update
            fresh[r, k] = (w + learn_rate * update).astype(bf16)

        @pl.when(i + p.slots < turns)
        def _():
            for copy in load_states(i + p.slots):
                copy.start()

    low, cw = p.low, p.cw
    recv = [b[f"recv{j}"] for j in range(low)]
    send = [b.get(f"send{j}") for j in range(low)]
    keep = [b.get(f"keep{j}") for j in range(low)]
    nxt, acc = b["nxt"], b["acc"]

    def order_of(o, k):
        order = list(range(low))
        if o == 0 and k % 2 and low > 1:
            order[0], order[1] = order[1], order[0]
        return order

    def pick(o, k, j, value):
        left = sorted(order_of(o, k)[j:], reverse=True)
        at = left.index(order_of(o, k)[j])
        return (ALL,) * at + (value,) + (ALL,) * (len(left) - 1 - at)

    def tail(k):
        return (ALL, pl.ds(k * cw, cw))

    def spot(o, j, k):
        return (o,) + (ALL,) * (low - 1 - j) + tail(k)

    flights = {}

    def launch(o, j, k, src):
        turn = order_of(o, k)[j]
        flights[o, j, k] = remote(src, recv[j].at[spot(o, j, k)], b["r_s"].at[o, j, k],
                                  b["r_r"].at[o, j, k], flip(2**turn), dp)
        flights[o, j, k].start()

    def multiply(o, k):
        t = behind[o]
        left = nh[pl.ds(t * 2, 2)].reshape(2 * rows, p.ff)
        product = jnp.dot(left, fresh[:, pl.ds(k * cw, cw)], preferred_element_type=f32).astype(bf16)
        nxt[(t,) + (ALL,) * low + tail(k)] = product.reshape((2,) * low + (p.few, cw))
        launch(o, 0, k, nxt.at[(t,) + pick(o, k, 0, 1 - bit[order_of(o, k)[0]]) + tail(k)])

    def combine(o, j, k):
        flights[o, j, k].wait_recv()

        def summed(index):
            if j == 0:
                mine = pick(o, k, 0, bit[order_of(o, k)[0]])
                full, i = [], iter(index)
                for m in mine:
                    full.append(next(i) if isinstance(m, slice) else m)
                kept = nxt[(behind[o],) + tuple(full) + tail(k)]
            else:
                kept = keep[j][(o,) + index + tail(k)]
            return kept.astype(f32) + recv[j][(o,) + index + tail(k)].astype(f32)

        if j < low - 1:
            turn = bit[order_of(o, k)[j + 1]]
            send[j + 1][spot(o, j + 1, k)] = summed(pick(o, k, j + 1, 1 - turn)).astype(bf16)
            launch(o, j + 1, k, send[j + 1].at[spot(o, j + 1, k)])
            keep[j + 1][spot(o, j + 1, k)] = summed(pick(o, k, j + 1, turn))
        else:
            acc[(behind[o],) + tail(k)] = summed(())

    tops = {}
    starts = [0]
    for j in range(p.high):
        starts.append(starts[j] + bit[low + p.high - 1 - j] * (chips >> (j + 1)))

    def top_launch(j, k):
        count = chips >> (j + 1)
        turn = low + p.high - 1 - j
        away = starts[j] + (1 - bit[turn]) * count
        b[f"top_send{j}"][(ALL,) + tail(k)] = acc[(pl.ds(away, count),) + tail(k)].astype(bf16)
        tops[j, k] = remote(b[f"top_send{j}"].at[(ALL,) + tail(k)], b[f"top_recv{j}"].at[(ALL,) + tail(k)],
                            b["t_s"].at[j, k], b["t_r"].at[j, k], flip(2**turn), dp)
        tops[j, k].start()

    def top_combine(j, k):
        count = chips >> (j + 1)
        tops[j, k].wait_recv()
        kept = acc[(pl.ds(starts[j + 1], count),) + tail(k)]
        total = kept + b[f"top_recv{j}"][(ALL,) + tail(k)].astype(f32)
        if j < p.high - 1:
            acc[(pl.ds(starts[j + 1], count),) + tail(k)] = total
            top_launch(j + 1, k)
        else:
            next_out[tail(k)] = total.reshape(p.few, cw).astype(bf16)

    def near(o, c):
        return remote(up.at[ahead[o], 1 - core, :, part_of(c)], b["up_in"].at[o, :, part_of(c)],
                      b["us_s"].at[o, c], b["us_r"].at[o, c], pipe, sib)

    def far(o, c):
        return remote(b["up_mid"].at[o, :, part_of(c)], b["up_far"].at[o, :, part_of(c)],
                      b["uf_s"].at[o, c], b["uf_r"].at[o, c], pipe, ahead[o] * 2 + core)

    def pieces_of(q):
        return range(q * p.pieces // p.halves, (q + 1) * p.pieces // p.halves)

    lead = min(2, p.chunks)
    for c in range(lead):
        for o in range(1, chips):
            hop(o, c).wait_recv()
            pass_on(o, c).start()
    own_g.wait()
    own_h.wait()
    for i in range(2):
        side[i].wait_recv()
    rest = p.chunks - p.early
    for q in range(p.halves):
        if q == 0:
            for c in passed[q]:
                c.wait_recv()

        def first_pass(c):
            @pl.when(c + lead < p.chunks)
            def _():
                for o in range(1, chips):
                    hop(o, c + lead).wait_recv()
                    pass_on(o, c + lead).start()

            for o in range(1, chips):
                pass_on(o, c).wait_recv()
            step(0, c)

        if q == 0:
            pl.loop(0, rest)(first_pass)
            for t in range(1, p.halves):
                for c in passed[t]:
                    c.wait_recv()

            @pl.loop(rest, p.chunks)
            def _(c):
                for t in range(1, p.halves):
                    load_w(t, c - rest).wait()
                up_chunk(c - rest)
                first_pass(c)

            own_n.wait()
            side[2].wait_recv()
        else:
            middle = p.chunks - p.chunks // 3
            before = list(pieces_of(q - 1))
            some = len(before) // 2

            @pl.loop(0, middle)
            def _(c):
                step(q, c)

            for k in before[:some]:
                combine(0, 0, k)

            @pl.loop(middle, p.chunks)
            def _(c):
                step(q, c)

            for k in before[some:]:
                combine(0, 0, k)

        for k in pieces_of(q):
            multiply(0, k)

    @pl.loop(p.early, p.chunks)
    def _(c):
        up_chunk(c)

    def finish(o, k):
        for level in range(1, low):
            combine(o, level, k)

    every = list(range(p.pieces))
    second_half = list(pieces_of(p.halves - 1))
    for k in every:
        if k not in second_half:
            finish(0, k)
    for o in range(1, chips):
        for i in range(2):
            later(o, i).wait_recv()
            pass_later(o, i).start()
        for i in range(2):
            pass_later(o, i).wait_recv()
        todo = second_half if o == 1 else every
        for k in every[:p.pieces // 2]:
            multiply(o, k)
        for k in todo:
            combine(o - 1, 0, k)
        for k in every[p.pieces // 2:]:
            multiply(o, k)
        if o < chips - 1:
            for k in todo:
                finish(o - 1, k)

    @pl.loop(0, p.chunks)
    def _(c):
        r = part_of(c)
        for o in range(1, chips):
            near(o, c).wait_recv()
            b["up_mid"][o, :, r] = (up[ahead[o], core, :, r].astype(f32)
                                    + b["up_in"][o, :, r].astype(f32)).astype(bf16)
            far(o, c).start()

    last, gap = chips - 1, 2
    for k in range(p.pieces + gap):
        if k == (p.pieces // 2 if last == 1 else 0):
            for t in todo:
                finish(last - 1, t)
        if k < p.pieces:
            combine(last, 0, k)
        if k >= gap:
            finish(last, k - gap)
            top_launch(0, k - gap)

    @pl.loop(0, p.chunks)
    def _(c):
        r = part_of(c)
        near(0, c).wait_recv()
        total = up[chip, core, :, r].astype(f32) + b["up_in"][0, :, r].astype(f32)
        for o in range(1, chips):
            far(o, c).wait_recv()
            total = total + b["up_far"][o, :, r].astype(f32)
        up_out[:, r] = total.astype(bf16)

    for j in range(p.high):
        for k in range(p.pieces):
            top_combine(j, k)

    relayed = [c for cs in passed.values() for c in cs]
    for c in list(cross.values()) + side + relayed + list(flights.values()) + list(tops.values()):
        c.wait_send()
    for o in range(1, chips):
        for i in range(2):
            later(o, i).wait_send()
            pass_later(o, i).wait_send()

    @pl.loop(0, p.chunks)
    def _(c):
        near(0, c).wait_send()
        for o in range(1, chips):
            hop(o, c).wait_send()
            pass_on(o, c).wait_send()
            near(o, c).wait_send()
            far(o, c).wait_send()


def place_kernel(a, b, c, x, y, z, sems):
    copies = [pltpu.make_async_copy(s, d, sems.at[i]) for i, (s, d) in enumerate(((a, x), (b, y), (c, z)))]
    for copy in copies:
        copy.start()
    for copy in copies:
        copy.wait()


def on_device(n_pipe, n_dp, grad_output, hidden, next_hidden, master, moment, second_moment):
    rows, ff = hidden.shape
    width = master.shape[1]
    p = Plan(n_pipe, n_dp, rows, ff, width)
    hbm = pl.BlockSpec(memory_space=pltpu.HBM)
    vmem = pl.BlockSpec(memory_space=pltpu.VMEM)
    shapes = [((ff, width), f32), ((rows, ff), bf16), ((p.few, width), bf16)]
    scratch = scratch_of(p)
    held = pl.pallas_call(
        functools.partial(whole_kernel, p, list(scratch)),
        out_shape=[pltpu.VMEM(s, t) for s, t in shapes],
        in_specs=[hbm] * 6,
        out_specs=[vmem] * 3,
        scratch_shapes=list(scratch.values()),
        compiler_params=pltpu.CompilerParams(
            collective_id=1, has_side_effects=True, vmem_limit_bytes=48 << 20
        ),
        cost_estimate=pl.CostEstimate(
            flops=6 * p.tokens * ff * width, bytes_accessed=16 * ff * width, transcendentals=ff * width
        ),
        name="whole_step",
    )(grad_output, hidden, next_hidden, master, moment, second_moment)
    held = [pltpu.with_memory_space_constraint(a, pltpu.VMEM) for a in held]
    return tuple(pl.pallas_call(
        place_kernel,
        out_shape=[jax.ShapeDtypeStruct(s, t) for s, t in shapes],
        in_specs=[vmem] * 3,
        out_specs=[hbm] * 3,
        scratch_shapes=[pltpu.SemaphoreType.DMA((3,))],
        compiler_params=pltpu.CompilerParams(has_side_effects=True, vmem_limit_bytes=1 << 20),
        name="place_outputs",
    )(*held))


def solution(mesh):
    in_specs = (
        P("dp", None),
        P("dp", "pipe"),
        P("dp", "pipe"),
        P("pipe", "dp"),
        P("pipe", "dp"),
        P("pipe", "dp"),
    )
    out_specs = (P("pipe", "dp"), P("dp", "pipe"), P("pipe", "dp"))

    def run(grad_output, hidden, next_hidden, master, moment, second_moment):
        f = functools.partial(on_device, mesh.shape["pipe"], mesh.shape["dp"])
        update, upstream, next_out = jax.shard_map(
            f, mesh=mesh, in_specs=in_specs, out_specs=out_specs, check_vma=False,
        )(grad_output, hidden, next_hidden, master, moment, second_moment)
        return update, upstream, next_out

    return run
```

```python
import functools
import math

import jax
import jax.numpy as jnp
from jax import lax
from jax.experimental import pallas as pl
from jax.experimental.pallas import tpu as pltpu
from jax.sharding import PartitionSpec as P

beta_one = 0.9
beta_two = 0.95
corr_one = 1.0 - 0.9**10
corr_two = 1.0 - 0.95**10
learn_rate = 0.005
decay_rate = 0.1
epsilon = 1e-08

f32 = jnp.float32
bf16 = jnp.bfloat16
MESH = pl.DeviceIdType.MESH
ALL = slice(None)


def remote(src, dst, send, recv, pipe, dp):
    return pltpu.make_async_remote_copy(
        src_ref=src, dst_ref=dst, send_sem=send, recv_sem=recv,
        device_id=(pipe, dp), device_id_type=MESH,
    )


def greet(partners):
    barrier = pltpu.get_barrier_semaphore()
    for partner in partners:
        pl.semaphore_signal(barrier, inc=1, device_id=partner, device_id_type=MESH)
    pl.semaphore_wait(barrier, len(partners))


def adam(w, m, s, grad):
    top = (-beta_one / corr_one) * m + (-(1.0 - beta_one) / corr_one) * grad
    var = (beta_two / corr_two) * s + ((1.0 - beta_two) / corr_two) * (grad * grad)
    root = lax.rsqrt(var)
    below = var * root + epsilon
    inverse = root * (2.0 - below * root)
    return top * inverse - decay_rate * w


class Plan:
    def __init__(self, n_pipe, n_dp, rows, ff, width):
        self.n_pipe, self.n_dp, self.rows, self.ff, self.width = n_pipe, n_dp, rows, ff, width
        self.chips = n_dp // 2
        self.tokens = n_dp * rows
        self.few = self.tokens // n_pipe
        self.share = 4 if n_pipe % 4 == 0 else 1
        self.low = int(math.log2(n_pipe // self.chips))
        self.high = int(math.log2(self.chips))
        self.chunk = 256 if ff % 256 == 0 else 128
        self.chunks = ff // self.chunk
        self.halves = 2 if width % 256 == 0 else 1
        self.hw = width // self.halves
        self.slots = min(4, self.chunks)
        self.far = self.chips - 1
        self.tile = 512 if self.hw % 512 == 0 else self.hw
        self.pieces = 8 if width % 2048 == 0 else 4 if width % 512 == 0 else 1
        self.cw = width // self.pieces


def scratch_of(p):
    dma = pltpu.SemaphoreType.DMA
    v = pltpu.VMEM
    mates = max(p.share - 1, 1)
    out = dict(
        w=v((p.ff, p.width), f32),
        m=v((p.slots, p.chunk, p.hw), f32),
        s=v((p.slots, p.chunk, p.hw), f32),
        fresh=v((p.ff, p.width), bf16),
        cols=v((p.n_dp, p.rows, p.width), bf16),
        h=v((p.n_dp, p.rows, p.ff), bf16),
        nh=v((p.n_dp, p.rows, p.ff), bf16),
        turned=v((p.chunk, p.tokens), bf16),
        up=v((p.chips, 2, p.rows, p.ff), bf16),
        up_in=v((p.chips, p.rows, p.ff), bf16),
        up_mid=v((p.far, p.rows, p.ff), bf16),
        up_far=v((p.far, p.rows, p.ff), bf16),
        nxt=v((p.chips,) + (2,) * p.low + (p.few, p.width), bf16),
        acc=v((p.chips, p.few, p.width), f32),
        loc=dma((3,)), m_l=dma((p.slots,)), w_l=dma((p.halves, p.chunks)), s_l=dma((p.slots,)),
        sib_s=dma((3,)), sib_r=dma((3,)),
        g_s=dma((p.far, 2)), g_r=dma((p.far, 2, p.halves)),
        gf_s=dma((p.far, mates)), gf_r=dma((p.far, 2, p.halves, mates)),
        h_s=dma((p.far,)), h_r=dma((p.far, p.chunks)),
        hf_s=dma((p.far,)), hf_r=dma((p.far, p.chunks)),
        n_s=dma((p.far,)), n_r=dma((p.far, 2)),
        nf_s=dma((p.far,)), nf_r=dma((p.far, 2)),
        us_s=dma((1,)), us_r=dma((p.chunks,)),
        uf_s=dma((p.far,)), uf_r=dma((p.far, p.chunks)),
        r_s=dma((p.chips, p.low)), r_r=dma((p.chips, p.low, p.pieces)),
        t_s=dma((p.high,)), t_r=dma((p.high, p.pieces)),
    )
    for j in range(p.low):
        shape = (p.chips,) + (2,) * (p.low - 1 - j) + (p.few, p.width)
        out[f"recv{j}"] = v(shape, bf16)
        if j:
            out[f"send{j}"] = v(shape, bf16)
            out[f"keep{j}"] = v(shape, f32)
    for j in range(p.high):
        shape = (p.chips >> (j + 1), p.few, p.width)
        out[f"top_send{j}"] = v(shape, bf16)
        out[f"top_recv{j}"] = v(shape, bf16)
    return out


def whole_kernel(p, names, g, hid, nhid, master, moment, second, upd, up_out, next_out, *refs):
    b = dict(zip(names, refs))
    cols, h, nh, fresh, up = (b[n] for n in ("cols", "h", "nh", "fresh", "up"))
    w_v, m_v, s_v = b["w"], b["m"], b["s"]
    pipe, dp = lax.axis_index("pipe"), lax.axis_index("dp")
    chips, rows, width, ch = p.chips, p.rows, p.width, p.chunk
    chip, core = dp // 2, dp % 2
    sib = chip * 2 + 1 - core
    ahead = [(chip + o) % chips for o in range(chips)]
    behind = [(chip + chips - o) % chips for o in range(chips)]
    bits = p.low + p.high
    bit = [(pipe // 2**i) % 2 for i in range(bits)]

    def flip(f):
        at = pipe
        for i in range(bits):
            if (f >> i) & 1:
                at = at + (1 - 2 * bit[i]) * 2**i
        return at

    def columns(d):
        return pl.ds(pl.multiple_of(d * width, width), width)

    def part_of(c):
        return pl.ds(pl.multiple_of(c * ch, ch), ch)

    own_g = pltpu.make_async_copy(g.at[:, columns(dp)], cols.at[dp], b["loc"].at[0])
    own_h = pltpu.make_async_copy(hid, h.at[dp], b["loc"].at[1])
    own_n = pltpu.make_async_copy(nhid, nh.at[dp], b["loc"].at[2])

    def side_of(q):
        return pl.ds(q * p.hw, p.hw)

    def load_w(q, c):
        at = (part_of(c), side_of(q))
        return pltpu.make_async_copy(master.at[at], w_v.at[at], b["w_l"].at[q, c])

    turns = p.halves * p.chunks

    def load_states(i):
        slot = i % p.slots
        at = (part_of(i % p.chunks), pl.ds(pl.multiple_of(i // p.chunks * p.hw, p.hw), p.hw))
        return [
            pltpu.make_async_copy(moment.at[at], m_v.at[slot], b["m_l"].at[slot]),
            pltpu.make_async_copy(second.at[at], s_v.at[slot], b["s_l"].at[slot]),
        ]

    for c in (own_g, own_h):
        c.start()
    for i in range(turns):
        load_w(i // p.chunks, i % p.chunks).start()
        if i < p.slots:
            for c in load_states(i):
                c.start()
        if i == p.chunks:
            own_n.start()

    partners = [(pipe, sib)]
    partners += [(pipe, ahead[o] * 2 + (core + e) % 2) for o in range(1, chips) for e in range(2)]
    flips = sorted(set(range(1, p.share)) | {2**i for i in range(bits)})
    partners += [(flip(f), dp) for f in flips]
    greet(partners)

    part = rows // p.share
    place = pipe % p.share

    def rows_of(at):
        return pl.ds(pl.multiple_of(at * part, part), part)

    def piece(d, q):
        return pl.ds(pl.multiple_of(d * width + q * p.hw, p.hw), p.hw)

    cross = {}
    for q in range(p.halves):
        for o in range(1, chips):
            for e in range(2):
                d = ahead[o] * 2 + (core + e) % 2
                cross[q, o, e] = remote(g.at[rows_of(place), piece(d, q)],
                                        cols.at[dp, rows_of(place), side_of(q)],
                                        b["g_s"].at[o - 1, e], b["g_r"].at[o - 1, e, q], pipe, d)
                cross[q, o, e].start()

    def shared(q, o, e, f):
        block = cols.at[behind[o] * 2 + (core + e) % 2, rows_of(place), side_of(q)]
        return remote(block, block, b["gf_s"].at[o - 1, f - 1], b["gf_r"].at[o - 1, e, q, f - 1], flip(f), dp)

    def hop(o, c):
        return remote(hid.at[:, part_of(c)], h.at[dp, :, part_of(c)],
                      b["h_s"].at[o - 1], b["h_r"].at[o - 1, c], pipe, ahead[o] * 2 + core)

    def pass_on(o, c):
        block = h.at[behind[o] * 2 + core, :, part_of(c)]
        return remote(block, block, b["hf_s"].at[o - 1], b["hf_r"].at[o - 1, c], pipe, sib)

    half = rows // 2

    def later(o, i):
        some = pl.ds(i * half, half)
        return remote(nhid.at[some], nh.at[dp, some], b["n_s"].at[o - 1], b["n_r"].at[o - 1, i],
                      pipe, ahead[o] * 2 + core)

    def pass_later(o, i):
        block = nh.at[behind[o] * 2 + core, pl.ds(i * half, half)]
        return remote(block, block, b["nf_s"].at[o - 1], b["nf_r"].at[o - 1, i], pipe, sib)

    side = [
        remote(g.at[:, columns(sib)], cols.at[dp], b["sib_s"].at[0], b["sib_r"].at[0], pipe, sib),
        remote(hid, h.at[dp], b["sib_s"].at[1], b["sib_r"].at[1], pipe, sib),
        remote(nhid, nh.at[dp], b["sib_s"].at[2], b["sib_r"].at[2], pipe, sib),
    ]
    for c in range(p.chunks):
        for o in range(1, chips):
            hop(o, c).start()
    for c in side:
        c.start()
    for o in range(1, chips):
        for i in range(2):
            later(o, i).start()

    passed = {q: [] for q in range(p.halves)}
    for key in cross:
        q, o, e = key
        cross[key].wait_recv()
        for f in range(1, p.share):
            c = shared(q, o, e, f)
            c.start()
            passed[q].append(c)

    def up_chunk(c):
        r = part_of(c)
        product = lax.dot_general(
            cols[...].reshape(p.tokens, width), w_v[r, :].astype(bf16),
            (((1,), (1,)), ((), ())), preferred_element_type=f32,
        ).astype(bf16)
        up[:, :, :, r] = product.reshape(chips, 2, rows, ch)
        near(c).start()

    def step(q, c):
        r = part_of(c)
        i = q * p.chunks + c
        slot = lax.rem(i, p.slots)
        load_w(q, c).wait()
        for copy in load_states(i):
            copy.wait()
        b["turned"][...] = h[:, :, r].reshape(p.tokens, ch).T
        for n in range(0, p.hw, p.tile):
            k = pl.ds(q * p.hw + n, p.tile)
            grad = jnp.dot(b["turned"][...], cols[:, :, k].reshape(p.tokens, p.tile),
                           preferred_element_type=f32)
            w = w_v[r, k]
            update = adam(w, m_v[slot, :, pl.ds(n, p.tile)], s_v[slot, :, pl.ds(n, p.tile)], grad)
            upd[r, k] = update
            fresh[r, k] = (w + learn_rate * update).astype(bf16)

        @pl.when(i + p.slots < turns)
        def _():
            for copy in load_states(i + p.slots):
                copy.start()

    low, cw = p.low, p.cw
    recv = [b[f"recv{j}"] for j in range(low)]
    send = [b.get(f"send{j}") for j in range(low)]
    keep = [b.get(f"keep{j}") for j in range(low)]
    nxt, acc = b["nxt"], b["acc"]

    def order_of(o, k):
        order = list(range(low))
        if o == 0 and k % 2 and low > 1:
            order[0], order[1] = order[1], order[0]
        return order

    def pick(o, k, j, value):
        left = sorted(order_of(o, k)[j:], reverse=True)
        at = left.index(order_of(o, k)[j])
        return (ALL,) * at + (value,) + (ALL,) * (len(left) - 1 - at)

    def tail(k):
        return (ALL, pl.ds(k * cw, cw))

    def spot(o, j, k):
        return (o,) + (ALL,) * (low - 1 - j) + tail(k)

    flights = {}

    def launch(o, j, k, src):
        turn = order_of(o, k)[j]
        flights[o, j, k] = remote(src, recv[j].at[spot(o, j, k)], b["r_s"].at[o, j],
                                  b["r_r"].at[o, j, k], flip(2**turn), dp)
        flights[o, j, k].start()

    def multiply(o, k):
        t = behind[o]
        left = nh[pl.ds(t * 2, 2)].reshape(2 * rows, p.ff)
        product = jnp.dot(left, fresh[:, pl.ds(k * cw, cw)], preferred_element_type=f32).astype(bf16)
        nxt[(t,) + (ALL,) * low + tail(k)] = product.reshape((2,) * low + (p.few, cw))
        launch(o, 0, k, nxt.at[(t,) + pick(o, k, 0, 1 - bit[order_of(o, k)[0]]) + tail(k)])

    def combine(o, j, k):
        flights[o, j, k].wait_recv()

        def summed(index):
            if j == 0:
                mine = pick(o, k, 0, bit[order_of(o, k)[0]])
                full, i = [], iter(index)
                for m in mine:
                    full.append(next(i) if isinstance(m, slice) else m)
                kept = nxt[(behind[o],) + tuple(full) + tail(k)]
            else:
                kept = keep[j][(o,) + index + tail(k)]
            return kept.astype(f32) + recv[j][(o,) + index + tail(k)].astype(f32)

        if j < low - 1:
            turn = bit[order_of(o, k)[j + 1]]
            send[j + 1][spot(o, j + 1, k)] = summed(pick(o, k, j + 1, 1 - turn)).astype(bf16)
            launch(o, j + 1, k, send[j + 1].at[spot(o, j + 1, k)])
            keep[j + 1][spot(o, j + 1, k)] = summed(pick(o, k, j + 1, turn))
        else:
            acc[(behind[o],) + tail(k)] = summed(())

    tops = {}
    starts = [0]
    for j in range(p.high):
        starts.append(starts[j] + bit[low + p.high - 1 - j] * (chips >> (j + 1)))

    def top_launch(j, k):
        count = chips >> (j + 1)
        turn = low + p.high - 1 - j
        away = starts[j] + (1 - bit[turn]) * count
        b[f"top_send{j}"][(ALL,) + tail(k)] = acc[(pl.ds(away, count),) + tail(k)].astype(bf16)
        tops[j, k] = remote(b[f"top_send{j}"].at[(ALL,) + tail(k)], b[f"top_recv{j}"].at[(ALL,) + tail(k)],
                            b["t_s"].at[j], b["t_r"].at[j, k], flip(2**turn), dp)
        tops[j, k].start()

    def top_combine(j, k):
        count = chips >> (j + 1)
        tops[j, k].wait_recv()
        kept = acc[(pl.ds(starts[j + 1], count),) + tail(k)]
        total = kept + b[f"top_recv{j}"][(ALL,) + tail(k)].astype(f32)
        if j < p.high - 1:
            acc[(pl.ds(starts[j + 1], count),) + tail(k)] = total
            top_launch(j + 1, k)
        else:
            next_out[tail(k)] = total.reshape(p.few, cw).astype(bf16)

    def near(c):
        return remote(up.at[:, 1 - core, :, part_of(c)], b["up_in"].at[:, :, part_of(c)],
                      b["us_s"].at[0], b["us_r"].at[c], pipe, sib)

    def far(o, c):
        return remote(b["up_mid"].at[o - 1, :, part_of(c)], b["up_far"].at[o - 1, :, part_of(c)],
                      b["uf_s"].at[o - 1], b["uf_r"].at[o - 1, c], pipe, ahead[o] * 2 + core)

    def pieces_of(q):
        return range(q * p.pieces // p.halves, (q + 1) * p.pieces // p.halves)

    lead = min(2, p.chunks)
    for c in range(lead):
        for o in range(1, chips):
            hop(o, c).wait_recv()
            pass_on(o, c).start()
    own_g.wait()
    own_h.wait()
    for i in range(2):
        side[i].wait_recv()
    for q in range(p.halves):
        for c in passed[q]:
            c.wait_recv()
        if q == 0:
            @pl.loop(0, p.chunks)
            def _(c):
                @pl.when(c + lead < p.chunks)
                def _():
                    for o in range(1, chips):
                        hop(o, c + lead).wait_recv()
                        pass_on(o, c + lead).start()

                for o in range(1, chips):
                    pass_on(o, c).wait_recv()
                step(0, c)

            own_n.wait()
            side[2].wait_recv()
        else:
            middle = p.chunks - p.chunks // 3
            before = list(pieces_of(q - 1))
            some = len(before) // 2

            @pl.loop(0, middle)
            def _(c):
                step(q, c)

            for k in before[:some]:
                combine(0, 0, k)

            @pl.loop(middle, p.chunks)
            def _(c):
                step(q, c)

            for k in before[some:]:
                combine(0, 0, k)

        for k in pieces_of(q):
            multiply(0, k)

    def finish(o, k):
        for level in range(1, low):
            combine(o, level, k)

    every = list(range(p.pieces))
    second_half = list(pieces_of(p.halves - 1))
    for k in every:
        if k not in second_half:
            finish(0, k)
    for o in range(1, chips):
        for i in range(2):
            later(o, i).wait_recv()
            pass_later(o, i).start()
        for i in range(2):
            pass_later(o, i).wait_recv()
        todo = second_half if o == 1 else every
        for k in every[:p.pieces // 2]:
            multiply(o, k)
        for k in todo:
            combine(o - 1, 0, k)
        for k in every[p.pieces // 2:]:
            multiply(o, k)
        if o < chips - 1:
            for k in todo:
                finish(o - 1, k)

    def up_part(first, end):
        @pl.loop(first, end)
        def _(c):
            up_chunk(c)

    def up_pass():
        @pl.loop(0, p.chunks)
        def _(c):
            r = part_of(c)
            near(c).wait_recv()
            for o in range(1, chips):
                b["up_mid"][o - 1, :, r] = (up[ahead[o], core, :, r].astype(f32)
                                            + b["up_in"][ahead[o], :, r].astype(f32)).astype(bf16)
                far(o, c).start()

    cut = [0, 3 * p.chunks // 7, 5 * p.chunks // 7, p.chunks]
    between = {i: functools.partial(up_part, cut[i], cut[i + 1]) for i in range(3)}
    between[4 if p.pieces > 4 else 3] = up_pass
    last, gap = chips - 1, 2
    for k in range(p.pieces + gap):
        if k in between:
            between[k]()
        if k == (p.pieces // 2 if last == 1 else 0):
            for t in todo:
                finish(last - 1, t)
        if k < p.pieces:
            combine(last, 0, k)
        if k >= gap:
            finish(last, k - gap)
            top_launch(0, k - gap)

    @pl.loop(0, p.chunks)
    def _(c):
        r = part_of(c)
        total = up[chip, core, :, r].astype(f32) + b["up_in"][chip, :, r].astype(f32)
        for o in range(1, chips):
            far(o, c).wait_recv()
            total = total + b["up_far"][o - 1, :, r].astype(f32)
        up_out[:, r] = total.astype(bf16)

    for j in range(p.high):
        for k in range(p.pieces):
            top_combine(j, k)

    def sent(block, sem):
        remote(block, block, sem, sem, pipe, sib).wait_send()

    for c in side:
        c.wait_send()
    for o in range(1, chips):
        sent(hid, b["h_s"].at[o - 1])
        sent(hid, b["hf_s"].at[o - 1])
        sent(hid, b["n_s"].at[o - 1])
        sent(hid, b["nf_s"].at[o - 1])
        sent(hid, b["uf_s"].at[o - 1])
        for e in range(2):
            sent(cols.at[0, rows_of(0)], b["g_s"].at[o - 1, e])
        for f in range(1, p.share):
            sent(cols.at[pl.ds(0, 2), rows_of(0)], b["gf_s"].at[o - 1, f - 1])
    sent(b["up_in"], b["us_s"].at[0])
    for o in range(chips):
        for j in range(low):
            sent(recv[j].at[o], b["r_s"].at[o, j])
    for j in range(p.high):
        sent(b[f"top_send{j}"], b["t_s"].at[j])


def place_kernel(a, b, c, x, y, z, sems):
    copies = [pltpu.make_async_copy(s, d, sems.at[i]) for i, (s, d) in enumerate(((a, x), (b, y), (c, z)))]
    for copy in copies:
        copy.start()
    for copy in copies:
        copy.wait()


def on_device(n_pipe, n_dp, grad_output, hidden, next_hidden, master, moment, second_moment):
    rows, ff = hidden.shape
    width = master.shape[1]
    p = Plan(n_pipe, n_dp, rows, ff, width)
    hbm = pl.BlockSpec(memory_space=pltpu.HBM)
    vmem = pl.BlockSpec(memory_space=pltpu.VMEM)
    shapes = [((ff, width), f32), ((rows, ff), bf16), ((p.few, width), bf16)]
    scratch = scratch_of(p)
    held = pl.pallas_call(
        functools.partial(whole_kernel, p, list(scratch)),
        out_shape=[pltpu.VMEM(s, t) for s, t in shapes],
        in_specs=[hbm] * 6,
        out_specs=[vmem] * 3,
        scratch_shapes=list(scratch.values()),
        compiler_params=pltpu.CompilerParams(
            collective_id=1, has_side_effects=True, vmem_limit_bytes=48 << 20
        ),
        cost_estimate=pl.CostEstimate(
            flops=6 * p.tokens * ff * width, bytes_accessed=16 * ff * width, transcendentals=ff * width
        ),
        name="whole_step",
    )(grad_output, hidden, next_hidden, master, moment, second_moment)
    held = [pltpu.with_memory_space_constraint(a, pltpu.VMEM) for a in held]
    return tuple(pl.pallas_call(
        place_kernel,
        out_shape=[jax.ShapeDtypeStruct(s, t) for s, t in shapes],
        in_specs=[vmem] * 3,
        out_specs=[hbm] * 3,
        scratch_shapes=[pltpu.SemaphoreType.DMA((3,))],
        compiler_params=pltpu.CompilerParams(has_side_effects=True, vmem_limit_bytes=1 << 20),
        name="place_outputs",
    )(*held))


def solution(mesh):
    in_specs = (
        P("dp", None),
        P("dp", "pipe"),
        P("dp", "pipe"),
        P("pipe", "dp"),
        P("pipe", "dp"),
        P("pipe", "dp"),
    )
    out_specs = (P("pipe", "dp"), P("dp", "pipe"), P("pipe", "dp"))

    def run(grad_output, hidden, next_hidden, master, moment, second_moment):
        f = functools.partial(on_device, mesh.shape["pipe"], mesh.shape["dp"])
        update, upstream, next_out = jax.shard_map(
            f, mesh=mesh, in_specs=in_specs, out_specs=out_specs, check_vma=False,
        )(grad_output, hidden, next_hidden, master, moment, second_moment)
        return update, upstream, next_out

    return run
```

```python
import functools
import math

import jax
import jax.numpy as jnp
from jax import lax
from jax.experimental import pallas as pl
from jax.experimental.pallas import tpu as pltpu
from jax.sharding import PartitionSpec as P

beta_one = 0.9
beta_two = 0.95
corr_one = 1.0 - 0.9**10
corr_two = 1.0 - 0.95**10
learn_rate = 0.005
decay_rate = 0.1
epsilon = 1e-08

f32 = jnp.float32
bf16 = jnp.bfloat16
MESH = pl.DeviceIdType.MESH
ALL = slice(None)


def remote(src, dst, send, recv, pipe, dp):
    return pltpu.make_async_remote_copy(
        src_ref=src, dst_ref=dst, send_sem=send, recv_sem=recv,
        device_id=(pipe, dp), device_id_type=MESH,
    )


def greet(partners):
    barrier = pltpu.get_barrier_semaphore()
    for partner in partners:
        pl.semaphore_signal(barrier, inc=1, device_id=partner, device_id_type=MESH)
    pl.semaphore_wait(barrier, len(partners))


def adam(w, m, s, grad):
    top = (-beta_one / corr_one) * m + (-(1.0 - beta_one) / corr_one) * grad
    var = (beta_two / corr_two) * s + ((1.0 - beta_two) / corr_two) * (grad * grad)
    root = lax.rsqrt(var)
    below = var * root + epsilon
    inverse = root * (2.0 - below * root)
    return top * inverse - decay_rate * w


class Plan:
    def __init__(self, n_pipe, n_dp, rows, ff, width):
        self.n_pipe, self.n_dp, self.rows, self.ff, self.width = n_pipe, n_dp, rows, ff, width
        self.chips = n_dp // 2
        self.tokens = n_dp * rows
        self.few = self.tokens // n_pipe
        self.share = 4 if n_pipe % 4 == 0 else 1
        self.low = int(math.log2(n_pipe // self.chips))
        self.high = int(math.log2(self.chips))
        self.chunk = 256 if ff % 256 == 0 else 128
        self.chunks = ff // self.chunk
        self.halves = 2 if width % 256 == 0 else 1
        self.hw = width // self.halves
        self.slots = min(4, self.chunks)
        self.far = self.chips - 1
        self.tile = 512 if self.hw % 512 == 0 else self.hw
        self.pieces = 4 if width % 512 == 0 else 1
        self.cw = width // self.pieces


def scratch_of(p):
    dma = pltpu.SemaphoreType.DMA
    v = pltpu.VMEM
    mates = max(p.share - 1, 1)
    out = dict(
        w=v((p.ff, p.width), f32),
        m=v((p.slots, p.chunk, p.hw), f32),
        s=v((p.slots, p.chunk, p.hw), f32),
        fresh=v((p.ff, p.width), bf16),
        cols=v((p.n_dp, p.rows, p.width), bf16),
        h=v((p.n_dp, p.rows, p.ff), bf16),
        nh=v((p.n_dp, p.rows, p.ff), bf16),
        turned=v((p.chunk, p.tokens), bf16),
        up=v((p.chips, 2, p.rows, p.ff), bf16),
        up_in=v((p.chips, p.rows, p.ff), bf16),
        up_mid=v((p.far, p.rows, p.ff), bf16),
        up_far=v((p.far, p.rows, p.ff), bf16),
        nxt=v((p.chips,) + (2,) * p.low + (p.few, p.width), bf16),
        acc=v((p.chips, p.few, p.width), f32),
        loc=dma((3,)), m_l=dma((p.slots,)), w_l=dma((p.halves, p.chunks)), s_l=dma((p.slots,)),
        sib_s=dma((3,)), sib_r=dma((3,)),
        g_s=dma((p.far, 2)), g_r=dma((p.far, 2, p.halves)),
        gf_s=dma((p.far, mates)), gf_r=dma((p.far, 2, p.halves, mates)),
        h_s=dma((p.far,)), h_r=dma((p.far, p.chunks)),
        hf_s=dma((p.far,)), hf_r=dma((p.far, p.chunks)),
        n_s=dma((p.far,)), n_r=dma((p.far, 2)),
        nf_s=dma((p.far,)), nf_r=dma((p.far, 2)),
        us_s=dma((1,)), us_r=dma((p.chunks,)),
        uf_s=dma((p.far,)), uf_r=dma((p.far, p.chunks)),
        r_s=dma((p.chips, p.low)), r_r=dma((p.chips, p.low, p.pieces)),
        t_s=dma((p.high,)), t_r=dma((p.high, p.pieces)),
    )
    for j in range(p.low):
        shape = (p.chips,) + (2,) * (p.low - 1 - j) + (p.few, p.width)
        out[f"recv{j}"] = v(shape, bf16)
        if j:
            out[f"send{j}"] = v(shape, bf16)
            out[f"keep{j}"] = v(shape, f32)
    for j in range(p.high):
        shape = (p.chips >> (j + 1), p.few, p.width)
        out[f"top_send{j}"] = v(shape, bf16)
        out[f"top_recv{j}"] = v(shape, bf16)
    return out


def whole_kernel(p, names, g, hid, nhid, master, moment, second, upd, up_out, next_out, *refs):
    b = dict(zip(names, refs))
    cols, h, nh, fresh, up = (b[n] for n in ("cols", "h", "nh", "fresh", "up"))
    w_v, m_v, s_v = b["w"], b["m"], b["s"]
    pipe, dp = lax.axis_index("pipe"), lax.axis_index("dp")
    chips, rows, width, ch = p.chips, p.rows, p.width, p.chunk
    chip, core = dp // 2, dp % 2
    sib = chip * 2 + 1 - core
    ahead = [(chip + o) % chips for o in range(chips)]
    behind = [(chip + chips - o) % chips for o in range(chips)]
    bits = p.low + p.high
    bit = [(pipe // 2**i) % 2 for i in range(bits)]

    def flip(f):
        at = pipe
        for i in range(bits):
            if (f >> i) & 1:
                at = at + (1 - 2 * bit[i]) * 2**i
        return at

    def columns(d):
        return pl.ds(pl.multiple_of(d * width, width), width)

    def part_of(c):
        return pl.ds(pl.multiple_of(c * ch, ch), ch)

    own_g = pltpu.make_async_copy(g.at[:, columns(dp)], cols.at[dp], b["loc"].at[0])
    own_h = pltpu.make_async_copy(hid, h.at[dp], b["loc"].at[1])
    own_n = pltpu.make_async_copy(nhid, nh.at[dp], b["loc"].at[2])

    def side_of(q):
        return pl.ds(q * p.hw, p.hw)

    def load_w(q, c):
        at = (part_of(c), side_of(q))
        return pltpu.make_async_copy(master.at[at], w_v.at[at], b["w_l"].at[q, c])

    turns = p.halves * p.chunks

    def load_states(i):
        slot = i % p.slots
        at = (part_of(i % p.chunks), pl.ds(pl.multiple_of(i // p.chunks * p.hw, p.hw), p.hw))
        return [
            pltpu.make_async_copy(moment.at[at], m_v.at[slot], b["m_l"].at[slot]),
            pltpu.make_async_copy(second.at[at], s_v.at[slot], b["s_l"].at[slot]),
        ]

    for c in (own_g, own_h):
        c.start()
    for i in range(turns):
        load_w(i // p.chunks, i % p.chunks).start()
        if i < p.slots:
            for c in load_states(i):
                c.start()
        if i == p.chunks:
            own_n.start()

    partners = [(pipe, sib)]
    partners += [(pipe, ahead[o] * 2 + (core + e) % 2) for o in range(1, chips) for e in range(2)]
    flips = sorted(set(range(1, p.share)) | {2**i for i in range(bits)})
    partners += [(flip(f), dp) for f in flips]
    greet(partners)

    part = rows // p.share
    place = pipe % p.share

    def rows_of(at):
        return pl.ds(pl.multiple_of(at * part, part), part)

    def piece(d, q):
        return pl.ds(pl.multiple_of(d * width + q * p.hw, p.hw), p.hw)

    cross = {}
    for q in range(p.halves):
        for o in range(1, chips):
            for e in range(2):
                d = ahead[o] * 2 + (core + e) % 2
                cross[q, o, e] = remote(g.at[rows_of(place), piece(d, q)],
                                        cols.at[dp, rows_of(place), side_of(q)],
                                        b["g_s"].at[o - 1, e], b["g_r"].at[o - 1, e, q], pipe, d)
                cross[q, o, e].start()

    def shared(q, o, e, f):
        block = cols.at[behind[o] * 2 + (core + e) % 2, rows_of(place), side_of(q)]
        return remote(block, block, b["gf_s"].at[o - 1, f - 1], b["gf_r"].at[o - 1, e, q, f - 1], flip(f), dp)

    def hop(o, c):
        return remote(hid.at[:, part_of(c)], h.at[dp, :, part_of(c)],
                      b["h_s"].at[o - 1], b["h_r"].at[o - 1, c], pipe, ahead[o] * 2 + core)

    def pass_on(o, c):
        block = h.at[behind[o] * 2 + core, :, part_of(c)]
        return remote(block, block, b["hf_s"].at[o - 1], b["hf_r"].at[o - 1, c], pipe, sib)

    half = rows // 2

    def later(o, i):
        some = pl.ds(i * half, half)
        return remote(nhid.at[some], nh.at[dp, some], b["n_s"].at[o - 1], b["n_r"].at[o - 1, i],
                      pipe, ahead[o] * 2 + core)

    def pass_later(o, i):
        block = nh.at[behind[o] * 2 + core, pl.ds(i * half, half)]
        return remote(block, block, b["nf_s"].at[o - 1], b["nf_r"].at[o - 1, i], pipe, sib)

    side = [
        remote(g.at[:, columns(sib)], cols.at[dp], b["sib_s"].at[0], b["sib_r"].at[0], pipe, sib),
        remote(hid, h.at[dp], b["sib_s"].at[1], b["sib_r"].at[1], pipe, sib),
        remote(nhid, nh.at[dp], b["sib_s"].at[2], b["sib_r"].at[2], pipe, sib),
    ]
    for c in range(p.chunks):
        for o in range(1, chips):
            hop(o, c).start()
    for c in side:
        c.start()
    for o in range(1, chips):
        for i in range(2):
            later(o, i).start()

    passed = {q: [] for q in range(p.halves)}
    for key in cross:
        q, o, e = key
        cross[key].wait_recv()
        for f in range(1, p.share):
            c = shared(q, o, e, f)
            c.start()
            passed[q].append(c)

    def up_chunk(c):
        r = part_of(c)
        product = lax.dot_general(
            cols[...].reshape(p.tokens, width), w_v[r, :].astype(bf16),
            (((1,), (1,)), ((), ())), preferred_element_type=f32,
        ).astype(bf16)
        up[:, :, :, r] = product.reshape(chips, 2, rows, ch)
        near(c).start()

    def step(q, c):
        r = part_of(c)
        i = q * p.chunks + c
        slot = lax.rem(i, p.slots)
        load_w(q, c).wait()
        for copy in load_states(i):
            copy.wait()
        b["turned"][...] = h[:, :, r].reshape(p.tokens, ch).T
        for n in range(0, p.hw, p.tile):
            k = pl.ds(q * p.hw + n, p.tile)
            grad = jnp.dot(b["turned"][...], cols[:, :, k].reshape(p.tokens, p.tile),
                           preferred_element_type=f32)
            w = w_v[r, k]
            update = adam(w, m_v[slot, :, pl.ds(n, p.tile)], s_v[slot, :, pl.ds(n, p.tile)], grad)
            upd[r, k] = update
            fresh[r, k] = (w + learn_rate * update).astype(bf16)

        @pl.when(i + p.slots < turns)
        def _():
            for copy in load_states(i + p.slots):
                copy.start()

    low, cw = p.low, p.cw
    recv = [b[f"recv{j}"] for j in range(low)]
    send = [b.get(f"send{j}") for j in range(low)]
    keep = [b.get(f"keep{j}") for j in range(low)]
    nxt, acc = b["nxt"], b["acc"]

    def order_of(o, k):
        order = list(range(low))
        if o == 0 and k % 2 and low > 1:
            order[0], order[1] = order[1], order[0]
        return order

    def pick(o, k, j, value):
        left = sorted(order_of(o, k)[j:], reverse=True)
        at = left.index(order_of(o, k)[j])
        return (ALL,) * at + (value,) + (ALL,) * (len(left) - 1 - at)

    def tail(k):
        return (ALL, pl.ds(k * cw, cw))

    def spot(o, j, k):
        return (o,) + (ALL,) * (low - 1 - j) + tail(k)

    flights = {}

    def launch(o, j, k, src):
        turn = order_of(o, k)[j]
        flights[o, j, k] = remote(src, recv[j].at[spot(o, j, k)], b["r_s"].at[o, j],
                                  b["r_r"].at[o, j, k], flip(2**turn), dp)
        flights[o, j, k].start()

    def multiply(o, k):
        t = behind[o]
        left = nh[pl.ds(t * 2, 2)].reshape(2 * rows, p.ff)
        product = jnp.dot(left, fresh[:, pl.ds(k * cw, cw)], preferred_element_type=f32).astype(bf16)
        nxt[(t,) + (ALL,) * low + tail(k)] = product.reshape((2,) * low + (p.few, cw))
        launch(o, 0, k, nxt.at[(t,) + pick(o, k, 0, 1 - bit[order_of(o, k)[0]]) + tail(k)])

    def combine(o, j, k):
        flights[o, j, k].wait_recv()

        def summed(index):
            if j == 0:
                mine = pick(o, k, 0, bit[order_of(o, k)[0]])
                full, i = [], iter(index)
                for m in mine:
                    full.append(next(i) if isinstance(m, slice) else m)
                kept = nxt[(behind[o],) + tuple(full) + tail(k)]
            else:
                kept = keep[j][(o,) + index + tail(k)]
            return kept.astype(f32) + recv[j][(o,) + index + tail(k)].astype(f32)

        if j < low - 1:
            turn = bit[order_of(o, k)[j + 1]]
            send[j + 1][spot(o, j + 1, k)] = summed(pick(o, k, j + 1, 1 - turn)).astype(bf16)
            launch(o, j + 1, k, send[j + 1].at[spot(o, j + 1, k)])
            keep[j + 1][spot(o, j + 1, k)] = summed(pick(o, k, j + 1, turn))
        else:
            acc[(behind[o],) + tail(k)] = summed(())

    tops = {}
    starts = [0]
    for j in range(p.high):
        starts.append(starts[j] + bit[low + p.high - 1 - j] * (chips >> (j + 1)))

    def top_launch(j, k):
        count = chips >> (j + 1)
        turn = low + p.high - 1 - j
        away = starts[j] + (1 - bit[turn]) * count
        b[f"top_send{j}"][(ALL,) + tail(k)] = acc[(pl.ds(away, count),) + tail(k)].astype(bf16)
        tops[j, k] = remote(b[f"top_send{j}"].at[(ALL,) + tail(k)], b[f"top_recv{j}"].at[(ALL,) + tail(k)],
                            b["t_s"].at[j], b["t_r"].at[j, k], flip(2**turn), dp)
        tops[j, k].start()

    def top_combine(j, k):
        count = chips >> (j + 1)
        tops[j, k].wait_recv()
        kept = acc[(pl.ds(starts[j + 1], count),) + tail(k)]
        total = kept + b[f"top_recv{j}"][(ALL,) + tail(k)].astype(f32)
        if j < p.high - 1:
            acc[(pl.ds(starts[j + 1], count),) + tail(k)] = total
            top_launch(j + 1, k)
        else:
            next_out[tail(k)] = total.reshape(p.few, cw).astype(bf16)

    def near(c):
        return remote(up.at[:, 1 - core, :, part_of(c)], b["up_in"].at[:, :, part_of(c)],
                      b["us_s"].at[0], b["us_r"].at[c], pipe, sib)

    def far(o, c):
        return remote(b["up_mid"].at[o - 1, :, part_of(c)], b["up_far"].at[o - 1, :, part_of(c)],
                      b["uf_s"].at[o - 1], b["uf_r"].at[o - 1, c], pipe, ahead[o] * 2 + core)

    def pieces_of(q):
        return range(q * p.pieces // p.halves, (q + 1) * p.pieces // p.halves)

    lead = min(2, p.chunks)
    for c in range(lead):
        for o in range(1, chips):
            hop(o, c).wait_recv()
            pass_on(o, c).start()
    own_g.wait()
    own_h.wait()
    for i in range(2):
        side[i].wait_recv()
    for q in range(p.halves):
        for c in passed[q]:
            c.wait_recv()
        if q == 0:
            @pl.loop(0, p.chunks)
            def _(c):
                @pl.when(c + lead < p.chunks)
                def _():
                    for o in range(1, chips):
                        hop(o, c + lead).wait_recv()
                        pass_on(o, c + lead).start()

                for o in range(1, chips):
                    pass_on(o, c).wait_recv()
                step(0, c)

            own_n.wait()
            side[2].wait_recv()
        else:
            middle = p.chunks - p.chunks // 3
            before = list(pieces_of(q - 1))
            some = len(before) // 2

            @pl.loop(0, middle)
            def _(c):
                step(q, c)

            for k in before[:some]:
                combine(0, 0, k)

            @pl.loop(middle, p.chunks)
            def _(c):
                step(q, c)

            for k in before[some:]:
                combine(0, 0, k)

        for k in pieces_of(q):
            multiply(0, k)

    def finish(o, k):
        for level in range(1, low):
            combine(o, level, k)

    every = list(range(p.pieces))
    second_half = list(pieces_of(p.halves - 1))
    for k in every:
        if k not in second_half:
            finish(0, k)
    for o in range(1, chips):
        for i in range(2):
            later(o, i).wait_recv()
            pass_later(o, i).start()
        for i in range(2):
            pass_later(o, i).wait_recv()
        todo = second_half if o == 1 else every
        for k in every[:p.pieces // 2]:
            multiply(o, k)
        for k in todo:
            combine(o - 1, 0, k)
        for k in every[p.pieces // 2:]:
            multiply(o, k)
        if o < chips - 1:
            for k in todo:
                finish(o - 1, k)

    def up_part(first, end):
        @pl.loop(first, end)
        def _(c):
            up_chunk(c)

    def up_pass():
        @pl.loop(0, p.chunks)
        def _(c):
            r = part_of(c)
            near(c).wait_recv()
            for o in range(1, chips):
                b["up_mid"][o - 1, :, r] = (up[ahead[o], core, :, r].astype(f32)
                                            + b["up_in"][ahead[o], :, r].astype(f32)).astype(bf16)
                far(o, c).start()

    cut = [0, 3 * p.chunks // 7, p.chunks]
    between = {i: functools.partial(up_part, cut[i], cut[i + 1]) for i in range(2)}
    between[2] = up_pass
    last, gap = chips - 1, 1
    for k in range(p.pieces + gap):
        if k in between:
            between[k]()
        if k == (p.pieces // 2 if last == 1 else 0):
            for t in todo:
                finish(last - 1, t)
        if k < p.pieces:
            combine(last, 0, k)
        if k >= gap:
            finish(last, k - gap)
            top_launch(0, k - gap)

    @pl.loop(0, p.chunks)
    def _(c):
        r = part_of(c)
        total = up[chip, core, :, r].astype(f32) + b["up_in"][chip, :, r].astype(f32)
        for o in range(1, chips):
            far(o, c).wait_recv()
            total = total + b["up_far"][o - 1, :, r].astype(f32)
        up_out[:, r] = total.astype(bf16)

    for j in range(p.high):
        for k in range(p.pieces):
            top_combine(j, k)

    def sent(block, sem):
        remote(block, block, sem, sem, pipe, sib).wait_send()

    for c in side:
        c.wait_send()
    for o in range(1, chips):
        sent(hid, b["h_s"].at[o - 1])
        sent(hid, b["hf_s"].at[o - 1])
        sent(hid, b["n_s"].at[o - 1])
        sent(hid, b["nf_s"].at[o - 1])
        sent(hid, b["uf_s"].at[o - 1])
        for e in range(2):
            sent(cols.at[0, rows_of(0)], b["g_s"].at[o - 1, e])
        for f in range(1, p.share):
            sent(cols.at[pl.ds(0, 2), rows_of(0)], b["gf_s"].at[o - 1, f - 1])
    sent(b["up_in"], b["us_s"].at[0])
    for o in range(chips):
        for j in range(low):
            sent(recv[j].at[o], b["r_s"].at[o, j])
    for j in range(p.high):
        sent(b[f"top_send{j}"], b["t_s"].at[j])


def place_kernel(a, b, c, x, y, z, sems):
    copies = [pltpu.make_async_copy(s, d, sems.at[i]) for i, (s, d) in enumerate(((a, x), (b, y), (c, z)))]
    for copy in copies:
        copy.start()
    for copy in copies:
        copy.wait()


def on_device(n_pipe, n_dp, grad_output, hidden, next_hidden, master, moment, second_moment):
    rows, ff = hidden.shape
    width = master.shape[1]
    p = Plan(n_pipe, n_dp, rows, ff, width)
    hbm = pl.BlockSpec(memory_space=pltpu.HBM)
    vmem = pl.BlockSpec(memory_space=pltpu.VMEM)
    shapes = [((ff, width), f32), ((rows, ff), bf16), ((p.few, width), bf16)]
    scratch = scratch_of(p)
    held = pl.pallas_call(
        functools.partial(whole_kernel, p, list(scratch)),
        out_shape=[pltpu.VMEM(s, t) for s, t in shapes],
        in_specs=[hbm] * 6,
        out_specs=[vmem] * 3,
        scratch_shapes=list(scratch.values()),
        compiler_params=pltpu.CompilerParams(
            collective_id=1, has_side_effects=True, vmem_limit_bytes=48 << 20
        ),
        cost_estimate=pl.CostEstimate(
            flops=6 * p.tokens * ff * width, bytes_accessed=16 * ff * width, transcendentals=ff * width
        ),
        name="whole_step",
    )(grad_output, hidden, next_hidden, master, moment, second_moment)
    held = [pltpu.with_memory_space_constraint(a, pltpu.VMEM) for a in held]
    return tuple(pl.pallas_call(
        place_kernel,
        out_shape=[jax.ShapeDtypeStruct(s, t) for s, t in shapes],
        in_specs=[vmem] * 3,
        out_specs=[hbm] * 3,
        scratch_shapes=[pltpu.SemaphoreType.DMA((3,))],
        compiler_params=pltpu.CompilerParams(has_side_effects=True, vmem_limit_bytes=1 << 20),
        name="place_outputs",
    )(*held))


def solution(mesh):
    in_specs = (
        P("dp", None),
        P("dp", "pipe"),
        P("dp", "pipe"),
        P("pipe", "dp"),
        P("pipe", "dp"),
        P("pipe", "dp"),
    )
    out_specs = (P("pipe", "dp"), P("dp", "pipe"), P("pipe", "dp"))

    def run(grad_output, hidden, next_hidden, master, moment, second_moment):
        f = functools.partial(on_device, mesh.shape["pipe"], mesh.shape["dp"])
        update, upstream, next_out = jax.shard_map(
            f, mesh=mesh, in_specs=in_specs, out_specs=out_specs, check_vma=False,
        )(grad_output, hidden, next_hidden, master, moment, second_moment)
        return update, upstream, next_out

    return run
```

```python
import functools
import math

import jax
import jax.numpy as jnp
from jax import lax
from jax.experimental import pallas as pl
from jax.experimental.pallas import tpu as pltpu
from jax.sharding import PartitionSpec as P

beta_one = 0.9
beta_two = 0.95
corr_one = 1.0 - 0.9**10
corr_two = 1.0 - 0.95**10
learn_rate = 0.005
decay_rate = 0.1
epsilon = 1e-08

f32 = jnp.float32
bf16 = jnp.bfloat16
MESH = pl.DeviceIdType.MESH
ALL = slice(None)


def remote(src, dst, send, recv, pipe, dp):
    return pltpu.make_async_remote_copy(
        src_ref=src, dst_ref=dst, send_sem=send, recv_sem=recv,
        device_id=(pipe, dp), device_id_type=MESH,
    )


def greet(partners):
    barrier = pltpu.get_barrier_semaphore()
    for partner in partners:
        pl.semaphore_signal(barrier, inc=1, device_id=partner, device_id_type=MESH)
    pl.semaphore_wait(barrier, len(partners))


def adam(w, m, s, grad):
    top = (-beta_one / corr_one) * m + (-(1.0 - beta_one) / corr_one) * grad
    var = (beta_two / corr_two) * s + ((1.0 - beta_two) / corr_two) * (grad * grad)
    root = lax.rsqrt(var)
    below = var * root + epsilon
    inverse = root * (2.0 - below * root)
    return top * inverse - decay_rate * w


class Plan:
    def __init__(self, n_pipe, n_dp, rows, ff, width):
        self.n_pipe, self.n_dp, self.rows, self.ff, self.width = n_pipe, n_dp, rows, ff, width
        self.chips = n_dp // 2
        self.tokens = n_dp * rows
        self.few = self.tokens // n_pipe
        self.share = 4 if n_pipe % 4 == 0 else 1
        self.low = int(math.log2(n_pipe // self.chips))
        self.high = int(math.log2(self.chips))
        self.chunk = 256 if ff % 256 == 0 else 128
        self.chunks = ff // self.chunk
        self.halves = 2 if width % 256 == 0 else 1
        self.hw = width // self.halves
        self.slots = min(4, self.chunks)
        self.far = self.chips - 1
        self.tile = 512 if self.hw % 512 == 0 else self.hw
        self.pieces = 4 if width % 512 == 0 else 1
        self.cw = width // self.pieces


def scratch_of(p):
    dma = pltpu.SemaphoreType.DMA
    v = pltpu.VMEM
    mates = max(p.share - 1, 1)
    out = dict(
        w=v((p.ff, p.width), f32),
        m=v((p.slots, p.chunk, p.hw), f32),
        s=v((p.slots, p.chunk, p.hw), f32),
        fresh=v((p.ff, p.width), bf16),
        cols=v((p.n_dp, p.rows, p.width), bf16),
        h=v((p.n_dp, p.rows, p.ff), bf16),
        nh=v((p.n_dp, p.rows, p.ff), bf16),
        turned=v((p.chunk, p.tokens), bf16),
        up=v((p.chips, 2, p.rows, p.ff), bf16),
        up_in=v((p.chips, p.rows, p.ff), bf16),
        up_mid=v((p.far, p.rows, p.ff), bf16),
        up_far=v((p.far, p.rows, p.ff), bf16),
        nxt=v((p.chips,) + (2,) * p.low + (p.few, p.width), bf16),
        acc=v((p.chips, p.few, p.width), f32),
        loc=dma((3,)), m_l=dma((p.slots,)), w_l=dma((p.halves, p.chunks)), s_l=dma((p.slots,)),
        sib_s=dma((3,)), sib_r=dma((3,)),
        g_s=dma((p.far, 2)), g_r=dma((p.far, 2, p.halves)),
        gf_s=dma((p.far, mates)), gf_r=dma((p.far, 2, p.halves, mates)),
        h_s=dma((p.far,)), h_r=dma((p.far, p.chunks)),
        hf_s=dma((p.far,)), hf_r=dma((p.far, p.chunks)),
        n_s=dma((p.far,)), n_r=dma((p.far, 2)),
        nf_s=dma((p.far,)), nf_r=dma((p.far, 2)),
        us_s=dma((1,)), us_r=dma((p.chunks,)),
        uf_s=dma((p.far,)), uf_r=dma((p.far, p.chunks)),
        r_s=dma((p.chips, p.low)), r_r=dma((p.chips, p.low, p.pieces)),
        t_s=dma((p.high,)), t_r=dma((p.high, p.pieces)),
    )
    for j in range(p.low):
        shape = (p.chips,) + (2,) * (p.low - 1 - j) + (p.few, p.width)
        out[f"recv{j}"] = v(shape, bf16)
        if j:
            out[f"send{j}"] = v(shape, bf16)
            out[f"keep{j}"] = v(shape, f32)
    for j in range(p.high):
        shape = (p.chips >> (j + 1), p.few, p.width)
        out[f"top_send{j}"] = v(shape, bf16)
        out[f"top_recv{j}"] = v(shape, bf16)
    return out


def whole_kernel(p, names, g, hid, nhid, master, moment, second, upd, up_out, next_out, *refs):
    b = dict(zip(names, refs))
    cols, h, nh, fresh, up = (b[n] for n in ("cols", "h", "nh", "fresh", "up"))
    w_v, m_v, s_v = b["w"], b["m"], b["s"]
    pipe, dp = lax.axis_index("pipe"), lax.axis_index("dp")
    chips, rows, width, ch = p.chips, p.rows, p.width, p.chunk
    chip, core = dp // 2, dp % 2
    sib = chip * 2 + 1 - core
    ahead = [(chip + o) % chips for o in range(chips)]
    behind = [(chip + chips - o) % chips for o in range(chips)]
    bits = p.low + p.high
    bit = [(pipe // 2**i) % 2 for i in range(bits)]

    def flip(f):
        at = pipe
        for i in range(bits):
            if (f >> i) & 1:
                at = at + (1 - 2 * bit[i]) * 2**i
        return at

    def columns(d):
        return pl.ds(pl.multiple_of(d * width, width), width)

    def part_of(c):
        return pl.ds(pl.multiple_of(c * ch, ch), ch)

    own_g = pltpu.make_async_copy(g.at[:, columns(dp)], cols.at[dp], b["loc"].at[0])
    own_h = pltpu.make_async_copy(hid, h.at[dp], b["loc"].at[1])
    own_n = pltpu.make_async_copy(nhid, nh.at[dp], b["loc"].at[2])

    def side_of(q):
        return pl.ds(q * p.hw, p.hw)

    def load_w(q, c):
        at = (part_of(c), side_of(q))
        return pltpu.make_async_copy(master.at[at], w_v.at[at], b["w_l"].at[q, c])

    turns = p.halves * p.chunks

    def load_states(i):
        slot = i % p.slots
        at = (part_of(i % p.chunks), pl.ds(pl.multiple_of(i // p.chunks * p.hw, p.hw), p.hw))
        return [
            pltpu.make_async_copy(moment.at[at], m_v.at[slot], b["m_l"].at[slot]),
            pltpu.make_async_copy(second.at[at], s_v.at[slot], b["s_l"].at[slot]),
        ]

    for c in (own_g, own_h):
        c.start()
    for i in range(turns):
        load_w(i // p.chunks, i % p.chunks).start()
        if i < p.slots:
            for c in load_states(i):
                c.start()
        if i == p.chunks:
            own_n.start()

    partners = [(pipe, sib)]
    partners += [(pipe, ahead[o] * 2 + (core + e) % 2) for o in range(1, chips) for e in range(2)]
    flips = sorted(set(range(1, p.share)) | {2**i for i in range(bits)})
    partners += [(flip(f), dp) for f in flips]
    greet(partners)

    part = rows // p.share
    place = pipe % p.share

    def rows_of(at):
        return pl.ds(pl.multiple_of(at * part, part), part)

    def piece(d, q):
        return pl.ds(pl.multiple_of(d * width + q * p.hw, p.hw), p.hw)

    cross = {}
    for q in range(p.halves):
        for o in range(1, chips):
            for e in range(2):
                d = ahead[o] * 2 + (core + e) % 2
                cross[q, o, e] = remote(g.at[rows_of(place), piece(d, q)],
                                        cols.at[dp, rows_of(place), side_of(q)],
                                        b["g_s"].at[o - 1, e], b["g_r"].at[o - 1, e, q], pipe, d)
                cross[q, o, e].start()

    def shared(q, o, e, f):
        block = cols.at[behind[o] * 2 + (core + e) % 2, rows_of(place), side_of(q)]
        return remote(block, block, b["gf_s"].at[o - 1, f - 1], b["gf_r"].at[o - 1, e, q, f - 1], flip(f), dp)

    def hop(o, c):
        return remote(hid.at[:, part_of(c)], h.at[dp, :, part_of(c)],
                      b["h_s"].at[o - 1], b["h_r"].at[o - 1, c], pipe, ahead[o] * 2 + core)

    def pass_on(o, c):
        block = h.at[behind[o] * 2 + core, :, part_of(c)]
        return remote(block, block, b["hf_s"].at[o - 1], b["hf_r"].at[o - 1, c], pipe, sib)

    half = rows // 2

    def later(o, i):
        some = pl.ds(i * half, half)
        return remote(nhid.at[some], nh.at[dp, some], b["n_s"].at[o - 1], b["n_r"].at[o - 1, i],
                      pipe, ahead[o] * 2 + core)

    def pass_later(o, i):
        block = nh.at[behind[o] * 2 + core, pl.ds(i * half, half)]
        return remote(block, block, b["nf_s"].at[o - 1], b["nf_r"].at[o - 1, i], pipe, sib)

    side = [
        remote(g.at[:, columns(sib)], cols.at[dp], b["sib_s"].at[0], b["sib_r"].at[0], pipe, sib),
        remote(hid, h.at[dp], b["sib_s"].at[1], b["sib_r"].at[1], pipe, sib),
        remote(nhid, nh.at[dp], b["sib_s"].at[2], b["sib_r"].at[2], pipe, sib),
    ]
    for c in range(p.chunks):
        for o in range(1, chips):
            hop(o, c).start()
    for c in side:
        c.start()
    for o in range(1, chips):
        for i in range(2):
            later(o, i).start()

    passed = {q: [] for q in range(p.halves)}
    for key in cross:
        q, o, e = key
        cross[key].wait_recv()
        for f in range(1, p.share):
            c = shared(q, o, e, f)
            c.start()
            passed[q].append(c)

    def up_chunk(c):
        r = part_of(c)
        product = lax.dot_general(
            cols[...].reshape(p.tokens, width), w_v[r, :].astype(bf16),
            (((1,), (1,)), ((), ())), preferred_element_type=f32,
        ).astype(bf16)
        up[:, :, :, r] = product.reshape(chips, 2, rows, ch)
        near(c).start()

    def step(q, c):
        r = part_of(c)
        i = q * p.chunks + c
        slot = lax.rem(i, p.slots)
        load_w(q, c).wait()
        for copy in load_states(i):
            copy.wait()
        b["turned"][...] = h[:, :, r].reshape(p.tokens, ch).T
        for n in range(0, p.hw, p.tile):
            k = pl.ds(q * p.hw + n, p.tile)
            grad = jnp.dot(b["turned"][...], cols[:, :, k].reshape(p.tokens, p.tile),
                           preferred_element_type=f32)
            w = w_v[r, k]
            update = adam(w, m_v[slot, :, pl.ds(n, p.tile)], s_v[slot, :, pl.ds(n, p.tile)], grad)
            upd[r, k] = update
            fresh[r, k] = (w + learn_rate * update).astype(bf16)

        @pl.when(i + p.slots < turns)
        def _():
            for copy in load_states(i + p.slots):
                copy.start()

    low, cw = p.low, p.cw
    recv = [b[f"recv{j}"] for j in range(low)]
    send = [b.get(f"send{j}") for j in range(low)]
    keep = [b.get(f"keep{j}") for j in range(low)]
    nxt, acc = b["nxt"], b["acc"]

    def order_of(o, k):
        return list(range(low))

    def pick(o, k, j, value):
        left = sorted(order_of(o, k)[j:], reverse=True)
        at = left.index(order_of(o, k)[j])
        return (ALL,) * at + (value,) + (ALL,) * (len(left) - 1 - at)

    def tail(k):
        return (ALL, pl.ds(k * cw, cw))

    def spot(o, j, k):
        return (o,) + (ALL,) * (low - 1 - j) + tail(k)

    flights = {}

    def launch(o, j, k, src):
        turn = order_of(o, k)[j]
        flights[o, j, k] = remote(src, recv[j].at[spot(o, j, k)], b["r_s"].at[o, j],
                                  b["r_r"].at[o, j, k], flip(2**turn), dp)
        flights[o, j, k].start()

    def multiply(o, k):
        t = behind[o]
        left = nh[pl.ds(t * 2, 2)].reshape(2 * rows, p.ff)
        product = jnp.dot(left, fresh[:, pl.ds(k * cw, cw)], preferred_element_type=f32).astype(bf16)
        nxt[(t,) + (ALL,) * low + tail(k)] = product.reshape((2,) * low + (p.few, cw))
        launch(o, 0, k, nxt.at[(t,) + pick(o, k, 0, 1 - bit[order_of(o, k)[0]]) + tail(k)])

    def combine(o, j, k):
        flights[o, j, k].wait_recv()

        def summed(index):
            if j == 0:
                mine = pick(o, k, 0, bit[order_of(o, k)[0]])
                full, i = [], iter(index)
                for m in mine:
                    full.append(next(i) if isinstance(m, slice) else m)
                kept = nxt[(behind[o],) + tuple(full) + tail(k)]
            else:
                kept = keep[j][(o,) + index + tail(k)]
            return kept.astype(f32) + recv[j][(o,) + index + tail(k)].astype(f32)

        if j < low - 1:
            turn = bit[order_of(o, k)[j + 1]]
            send[j + 1][spot(o, j + 1, k)] = summed(pick(o, k, j + 1, 1 - turn)).astype(bf16)
            launch(o, j + 1, k, send[j + 1].at[spot(o, j + 1, k)])
            keep[j + 1][spot(o, j + 1, k)] = summed(pick(o, k, j + 1, turn))
        else:
            acc[(behind[o],) + tail(k)] = summed(())

    tops = {}
    starts = [0]
    for j in range(p.high):
        starts.append(starts[j] + bit[low + p.high - 1 - j] * (chips >> (j + 1)))

    def top_launch(j, k):
        count = chips >> (j + 1)
        turn = low + p.high - 1 - j
        away = starts[j] + (1 - bit[turn]) * count
        b[f"top_send{j}"][(ALL,) + tail(k)] = acc[(pl.ds(away, count),) + tail(k)].astype(bf16)
        tops[j, k] = remote(b[f"top_send{j}"].at[(ALL,) + tail(k)], b[f"top_recv{j}"].at[(ALL,) + tail(k)],
                            b["t_s"].at[j], b["t_r"].at[j, k], flip(2**turn), dp)
        tops[j, k].start()

    def top_combine(j, k):
        count = chips >> (j + 1)
        tops[j, k].wait_recv()
        kept = acc[(pl.ds(starts[j + 1], count),) + tail(k)]
        total = kept + b[f"top_recv{j}"][(ALL,) + tail(k)].astype(f32)
        if j < p.high - 1:
            acc[(pl.ds(starts[j + 1], count),) + tail(k)] = total
            top_launch(j + 1, k)
        else:
            next_out[tail(k)] = total.reshape(p.few, cw).astype(bf16)

    def near(c):
        return remote(up.at[:, 1 - core, :, part_of(c)], b["up_in"].at[:, :, part_of(c)],
                      b["us_s"].at[0], b["us_r"].at[c], pipe, sib)

    def far(o, c):
        return remote(b["up_mid"].at[o - 1, :, part_of(c)], b["up_far"].at[o - 1, :, part_of(c)],
                      b["uf_s"].at[o - 1], b["uf_r"].at[o - 1, c], pipe, ahead[o] * 2 + core)

    def pieces_of(q):
        return range(q * p.pieces // p.halves, (q + 1) * p.pieces // p.halves)

    lead = min(2, p.chunks)
    for c in range(lead):
        for o in range(1, chips):
            hop(o, c).wait_recv()
            pass_on(o, c).start()
    own_g.wait()
    own_h.wait()
    for i in range(2):
        side[i].wait_recv()
    for q in range(p.halves):
        for c in passed[q]:
            c.wait_recv()
        if q == 0:
            @pl.loop(0, p.chunks)
            def _(c):
                @pl.when(c + lead < p.chunks)
                def _():
                    for o in range(1, chips):
                        hop(o, c + lead).wait_recv()
                        pass_on(o, c + lead).start()

                for o in range(1, chips):
                    pass_on(o, c).wait_recv()
                step(0, c)

            own_n.wait()
            side[2].wait_recv()
        else:
            middle = p.chunks - p.chunks // 3
            before = list(pieces_of(q - 1))
            some = len(before) // 2

            @pl.loop(0, middle)
            def _(c):
                step(q, c)

            for k in before[:some]:
                combine(0, 0, k)

            @pl.loop(middle, p.chunks)
            def _(c):
                step(q, c)

            for k in before[some:]:
                combine(0, 0, k)

        for k in pieces_of(q):
            multiply(0, k)

    def finish(o, k):
        for level in range(1, low):
            combine(o, level, k)

    every = list(range(p.pieces))
    second_half = list(pieces_of(p.halves - 1))
    for k in every:
        if k not in second_half:
            finish(0, k)
    for o in range(1, chips):
        for i in range(2):
            later(o, i).wait_recv()
            pass_later(o, i).start()
        for i in range(2):
            pass_later(o, i).wait_recv()
        todo = second_half if o == 1 else every
        for k in every[:p.pieces // 2]:
            multiply(o, k)
        for k in todo:
            combine(o - 1, 0, k)
        for k in every[p.pieces // 2:]:
            multiply(o, k)
        if o < chips - 1:
            for k in todo:
                finish(o - 1, k)

    def up_part(first, end):
        @pl.loop(first, end)
        def _(c):
            up_chunk(c)

    def up_pass():
        @pl.loop(0, p.chunks)
        def _(c):
            r = part_of(c)
            near(c).wait_recv()
            for o in range(1, chips):
                b["up_mid"][o - 1, :, r] = (up[ahead[o], core, :, r].astype(f32)
                                            + b["up_in"][ahead[o], :, r].astype(f32)).astype(bf16)
                far(o, c).start()

    cut = [0, 3 * p.chunks // 7, p.chunks]
    between = {i: functools.partial(up_part, cut[i], cut[i + 1]) for i in range(2)}
    between[2] = up_pass
    last, gap = chips - 1, 1
    for k in range(p.pieces + gap):
        if k in between:
            between[k]()
        if k == (p.pieces // 2 if last == 1 else 0):
            for t in todo:
                finish(last - 1, t)
        if k < p.pieces:
            combine(last, 0, k)
        if k >= gap:
            finish(last, k - gap)
            top_launch(0, k - gap)

    @pl.loop(0, p.chunks)
    def _(c):
        r = part_of(c)
        total = up[chip, core, :, r].astype(f32) + b["up_in"][chip, :, r].astype(f32)
        for o in range(1, chips):
            far(o, c).wait_recv()
            total = total + b["up_far"][o - 1, :, r].astype(f32)
        up_out[:, r] = total.astype(bf16)

    for j in range(p.high):
        for k in range(p.pieces):
            top_combine(j, k)

    def sent(block, sem):
        remote(block, block, sem, sem, pipe, sib).wait_send()

    for c in side:
        c.wait_send()
    for o in range(1, chips):
        sent(hid, b["h_s"].at[o - 1])
        sent(hid, b["hf_s"].at[o - 1])
        sent(hid, b["n_s"].at[o - 1])
        sent(hid, b["nf_s"].at[o - 1])
        sent(hid, b["uf_s"].at[o - 1])
        for e in range(2):
            sent(cols.at[0, rows_of(0)], b["g_s"].at[o - 1, e])
        for f in range(1, p.share):
            sent(cols.at[pl.ds(0, 2), rows_of(0)], b["gf_s"].at[o - 1, f - 1])
    sent(b["up_in"], b["us_s"].at[0])
    for o in range(chips):
        for j in range(low):
            sent(recv[j].at[o], b["r_s"].at[o, j])
    for j in range(p.high):
        sent(b[f"top_send{j}"], b["t_s"].at[j])


def place_kernel(a, b, c, x, y, z, sems):
    copies = [pltpu.make_async_copy(s, d, sems.at[i]) for i, (s, d) in enumerate(((a, x), (b, y), (c, z)))]
    for copy in copies:
        copy.start()
    for copy in copies:
        copy.wait()


def on_device(n_pipe, n_dp, grad_output, hidden, next_hidden, master, moment, second_moment):
    rows, ff = hidden.shape
    width = master.shape[1]
    p = Plan(n_pipe, n_dp, rows, ff, width)
    hbm = pl.BlockSpec(memory_space=pltpu.HBM)
    vmem = pl.BlockSpec(memory_space=pltpu.VMEM)
    shapes = [((ff, width), f32), ((rows, ff), bf16), ((p.few, width), bf16)]
    scratch = scratch_of(p)
    held = pl.pallas_call(
        functools.partial(whole_kernel, p, list(scratch)),
        out_shape=[pltpu.VMEM(s, t) for s, t in shapes],
        in_specs=[hbm] * 6,
        out_specs=[vmem] * 3,
        scratch_shapes=list(scratch.values()),
        compiler_params=pltpu.CompilerParams(
            collective_id=1, has_side_effects=True, vmem_limit_bytes=48 << 20
        ),
        cost_estimate=pl.CostEstimate(
            flops=6 * p.tokens * ff * width, bytes_accessed=16 * ff * width, transcendentals=ff * width
        ),
        name="whole_step",
    )(grad_output, hidden, next_hidden, master, moment, second_moment)
    held = [pltpu.with_memory_space_constraint(a, pltpu.VMEM) for a in held]
    return tuple(pl.pallas_call(
        place_kernel,
        out_shape=[jax.ShapeDtypeStruct(s, t) for s, t in shapes],
        in_specs=[vmem] * 3,
        out_specs=[hbm] * 3,
        scratch_shapes=[pltpu.SemaphoreType.DMA((3,))],
        compiler_params=pltpu.CompilerParams(has_side_effects=True, vmem_limit_bytes=1 << 20),
        name="place_outputs",
    )(*held))


def solution(mesh):
    in_specs = (
        P("dp", None),
        P("dp", "pipe"),
        P("dp", "pipe"),
        P("pipe", "dp"),
        P("pipe", "dp"),
        P("pipe", "dp"),
    )
    out_specs = (P("pipe", "dp"), P("dp", "pipe"), P("pipe", "dp"))

    def run(grad_output, hidden, next_hidden, master, moment, second_moment):
        f = functools.partial(on_device, mesh.shape["pipe"], mesh.shape["dp"])
        update, upstream, next_out = jax.shard_map(
            f, mesh=mesh, in_specs=in_specs, out_specs=out_specs, check_vma=False,
        )(grad_output, hidden, next_hidden, master, moment, second_moment)
        return update, upstream, next_out

    return run
```
